32 devices in a mesh: aux: 4 (over z), pair: 8 (over y, x, core).
Axes of the slice: x: 2, y: 2, z: 4, core: 2. Of those that a mesh axis runs over, the one named last changes fastest.
Arguments:
- b_three: bfloat16 [4096, 2048], P('pair', 'aux'), may hold values from -0.13183594 to 0.13183594
- metric: bfloat16 [2048, 2048], P(None, 'aux'), may hold values from -1 to 2
- aux_map: int32 [64, 32], P('pair', 'aux'), may hold values 0 or 1
- domains: int32 [80, 4], replicated, may hold values from 0 to 63, as said below
- counts: int32 [80], P('pair'), may hold values from 1 to 4, as said below
Outputs:
- pair_integrals: float32 [80, 256, 256], P('pair', 'aux')
The draws below stay inside these ranges and needn't reach their ends.
Inputs may be any that keep to these rules, and one draw needn't show every extreme that they name: `domains`: of the 40 slots of the pairs of one index of pair (pairs q * 10 to (q + 1) * 10 - 1), at most 5 name blocks held by one index of pair (blocks o * 8 to (o + 1) * 8 - 1), and exactly 5 for some such index in every draw. `counts`: slots at or past a pair's count are padding.
All inputs are finite; a program needn't handle non-finite values. No bound on the sum of `aux_map` on one device may be relied on, other than what follows from the above.
Results may differ from the reference program's by a relative error of at most 0.00079.
Values may be sent and summed in bfloat16 or wider, within the bound.
A program may use at most 64 MiB of HBM per device.

```python
import jax
import jax.numpy as jnp
from jax import lax

AUXW = 64
CW = 64
DMAX = 4
DB_DEV = 8
PAIR_DEV = 10
NAB = 32
NA = 2048
NDB = 64
NPAIRS = 80
SLOTS = 40
CAP = 5
N_PAIR = 8


def draw_metric(key, part):
    noise = jax.random.normal(key, (NA, NA), jnp.float32)
    return (jnp.eye(NA, dtype=jnp.float32) + 0.5 * noise * NA ** (-0.5)).astype(jnp.bfloat16)


def draw_domains(key, part):
    device_keys = jax.random.split(jax.random.fold_in(key, 11), N_PAIR)

    def one_device(sub_key):
        shuffled = jax.random.permutation(sub_key, CAP * N_PAIR)
        return (shuffled[:SLOTS] % N_PAIR).astype(jnp.int32)
    owners = jax.vmap(one_device)(device_keys)
    local_block = jax.random.randint(jax.random.fold_in(key, 12), (N_PAIR, SLOTS), 0, DB_DEV)
    return (owners * DB_DEV + local_block).reshape(NPAIRS, DMAX).astype(jnp.int32)


def draw_counts(key, part):
    device_level = jax.random.randint(jax.random.fold_in(key, 21), (N_PAIR, 1), 1, DMAX + 1)
    raw_counts = jax.random.randint(jax.random.fold_in(key, 22), (N_PAIR, PAIR_DEV), 1, DMAX + 1)
    counts = jnp.minimum(raw_counts, device_level).reshape(NPAIRS)
    full_pair = jax.random.randint(jax.random.fold_in(key, 23), (), 0, NPAIRS)
    return counts.at[full_pair].set(DMAX).astype(jnp.int32)


def place_ends(result, rng, smallest, largest):
    longest = result.shape.index(max(result.shape))
    spots = []
    for shift in (0, 1):
        where = [jax.random.randint(jax.random.fold_in(rng, axis), (), 0, length) for axis, length in enumerate(result.shape)]
        where[longest] = (where[longest] + shift) % result.shape[longest]
        spots.append(tuple(where))
    return result.at[spots[0]].set(smallest).at[spots[1]].set(largest)


def shard_levels(own_key, shape, pieces, low, largest):
    gain = 1.0
    for dim, shards_of in pieces:
        draws = jax.random.uniform(jax.random.fold_in(jax.random.fold_in(own_key, 6), dim), (shards_of,), jnp.float32, low / len(pieces), largest / len(pieces))
        gain = gain * jnp.repeat(jnp.exp(draws), shape[dim] // shards_of).reshape((-1,) + (1,) * (len(shape) - 1 - dim))
    return gain


def gaussian(key, shape, width, most, cuts=(), kind=jnp.bfloat16):
    entries = jax.random.normal(key, shape, jnp.float32) * width
    if len(cuts) > 0:
        entries = shard_levels(key, shape, cuts, -0.22, 0.18) * entries
    return jnp.clip(entries, min=-most, max=most).astype(kind)


def setup_inputs(seed: int = 0) -> dict:
    keys = jax.random.split(jax.random.key(seed), 6)
    return {
        "b_three": gaussian(keys[0], (NDB * CW, NA), (NA ** -0.5), 0.13183594, ((0, 8), (1, 4))),
        "metric": draw_metric(jax.random.fold_in(keys[5], 71), 0),
        "aux_map": place_ends((jax.random.randint(keys[2], (NDB, NAB), 0, 4) < 3).astype(jnp.int32), jax.random.fold_in(keys[2], 1), 0, 1),
        "domains": draw_domains(jax.random.fold_in(keys[5], 71), 0),
        "counts": draw_counts(jax.random.fold_in(keys[5], 71), 0),
    }


def reference(b_three, metric, aux_map, domains, counts):
    keep_mask = aux_map.astype(jnp.bfloat16)
    row_total, aux_total = b_three.shape
    masked = (b_three.reshape(NDB, CW, NAB, AUXW) * keep_mask[:, None, :, None]).reshape(row_total, aux_total)
    fitted = jnp.dot(masked, metric, preferred_element_type=jnp.float32).astype(jnp.bfloat16)
    block_table = fitted.reshape(NDB, CW, aux_total)
    slot_of = jnp.arange(DMAX * CW, dtype=jnp.int32) // CW

    def one_pair(entry):
        block_names, live_count = entry
        stacked = block_table[block_names].reshape(DMAX * CW, aux_total).astype(jnp.float32)
        product = jnp.dot(stacked, stacked.T, preferred_element_type=jnp.float32)
        live_rows = slot_of < live_count
        return jnp.where(live_rows[:, None] & live_rows[None, :], product, jnp.zeros_like(product))

    return lax.map(one_pair, (domains, counts))
```

```python
import functools

import jax
import jax.numpy as jnp
from jax import lax
from jax.experimental import pallas as pl
from jax.experimental.pallas import tpu as pltpu
from jax.sharding import PartitionSpec as P

MESH = pl.DeviceIdType.MESH


def kernel(n, n_pair, b_ref, metric_ref, dom_ref, cnt_ref, out_ref,
           b_all, table, g_send, g_recv, d_own, d_recv,
           r_s, r_r, l_s, l_r, p_s, p_r, f_s, f_r, g_s, g_r, d_s, d_r):
    chunks, rows, depth = b_ref.shape
    pairs, slab, width = out_ref.shape
    slots = dom_ref.shape[1]
    chips = n_pair // 2
    z = lax.axis_index("aux")
    q = lax.axis_index("pair")
    core = lax.rem(q, 2)
    chip = q // 2
    partner = q + 1 - 2 * core
    has_right = z + 1 < n
    has_left = z > 0

    def chip_at(k):
        return lax.rem(chip + k + chips, chips) * 2 + core

    barrier = pltpu.get_barrier_semaphore()
    for k in range(1, n):
        pl.semaphore_signal(barrier, inc=1, device_id=(lax.rem(z + k, n), q), device_id_type=MESH)
    for k in range(1, chips):
        pl.semaphore_signal(barrier, inc=1, device_id=(z, chip_at(k)), device_id_type=MESH)
    pl.semaphore_signal(barrier, inc=1, device_id=(z, partner), device_id_type=MESH)
    pl.semaphore_wait(barrier, n + chips - 1)

    def remote(src, dst, send, recv, device):
        return pltpu.make_async_remote_copy(
            src_ref=src, dst_ref=dst, send_sem=send, recv_sem=recv, device_id=device, device_id_type=MESH)

    def along(h, c, right):
        step = 1 if right else -1
        origin = z - step * h
        send, recv = (r_s, r_r) if right else (l_s, l_r)
        src = b_ref.at[c] if h == 0 else b_all.at[origin, c]
        return remote(src, b_all.at[origin, c], send.at[h, c], recv.at[h, c], (z + step, q))

    def arrival(h, c, right):
        recv = r_r if right else l_r
        origin = z - 1 - h if right else z + 1 + h
        return remote(b_ref.at[c], b_all.at[origin, c], recv.at[h, c], recv.at[h, c], (z, partner))

    def own_chunk(c):
        for right in (True, False):
            @pl.when(has_right if right else has_left)
            def _():
                along(0, c, right).start()

    def relay(h, c):
        for right in (True, False):
            came = z - h >= 0 if right else z + h < n

            @pl.when(came)
            def _():
                arrival(h - 1, c, right).wait_recv()

                if h < n - 1:
                    @pl.when(has_right if right else has_left)
                    def _():
                        along(h, c, right).start()

    def spread(k, c):
        target = partner if k == 0 else chip_at(k)
        return remote(table.at[q, c], table.at[q, c], p_s.at[k, c], p_r.at[k, c], (z, target))

    def forward(k, c):
        origin = chip_at(-k)
        return remote(table.at[origin, c], table.at[origin, c], f_s.at[k, c], f_r.at[k, c], (z, partner))

    def fit(c):
        total = jnp.dot(b_ref[c], metric_ref[pl.ds(pl.multiple_of(z * depth, depth), depth), :],
                        preferred_element_type=jnp.float32)
        for k in range(1, n):
            origin = lax.rem(z + k, n)
            total += jnp.dot(b_all[origin, c],
                             metric_ref[pl.ds(pl.multiple_of(origin * depth, depth), depth), :],
                             preferred_element_type=jnp.float32)
        table[q, c] = total.astype(table.dtype)
        for k in list(range(1, chips)) + [0]:
            spread(k, c).start()

    def pass_on(c):
        for k in range(1, chips):
            spread_in = remote(table.at[chip_at(-k), c], table.at[chip_at(-k), c],
                               p_s.at[k, c], p_r.at[k, c], (z, partner))
            spread_in.wait_recv()
            forward(k, c).start()

    own_chunk(0)

    def stage(step, carry):
        @pl.when(step + 1 < chunks)
        def _():
            own_chunk(step + 1)
        for h in range(1, n):
            @pl.when((step + 1 >= h) & (step + 1 - h < chunks))
            def _():
                relay(h, step + 1 - h)

        @pl.when((step + 2 >= n) & (step + 2 - n < chunks))
        def _():
            fit(step + 2 - n)

        @pl.when((step >= n) & (step - n < chunks))
        def _():
            pass_on(step - n)
        return carry

    lax.fori_loop(0, chunks + n, stage, 0)

    def finish(c, carry):
        remote(table.at[partner, c], table.at[partner, c], p_s.at[0, c], p_r.at[0, c],
               (z, partner)).wait_recv()
        for k in range(1, chips):
            origin = chip_at(-k) + 1 - 2 * core
            remote(table.at[origin, c], table.at[origin, c], f_s.at[k, c], f_r.at[k, c],
                   (z, partner)).wait_recv()
        return carry

    lax.fori_loop(0, chunks, finish, 0)

    row_of = lax.broadcasted_iota(jnp.int32, (width, width), 0)
    col_of = lax.broadcasted_iota(jnp.int32, (width, width), 1)

    def gram_copy(k, p):
        return remote(g_send.at[lax.rem(z + k, n), p], g_recv.at[k - 1, p],
                      g_s.at[k - 1, p], g_r.at[k - 1, p], (lax.rem(z + k, n), q))

    def gram(p, carry):
        blocks = []
        for s in range(slots):
            name = dom_ref[q * pairs + p, s]
            blocks.append(table[name // chunks, lax.rem(name, chunks)])
        stack = jnp.concatenate(blocks, axis=0)
        full = lax.dot_general(stack, stack, (((1,), (1,)), ((), ())), preferred_element_type=jnp.float32)
        d_own[p] = jnp.sum(jnp.where(row_of == col_of, full, 0.0), axis=0, keepdims=True)
        for d in range(n):
            part = full[d * slab:(d + 1) * slab]

            @pl.when(z == d)
            def _():
                out_ref[p] = part

            @pl.when(z != d)
            def _():
                g_send[d, p] = part.astype(g_send.dtype)
        for k in range(1, n):
            gram_copy(k, p).start()
        return carry

    lax.fori_loop(0, pairs, gram, 0)

    def diag_copy(k):
        return remote(d_own, d_recv.at[k - 1], d_s.at[k - 1], d_r.at[k - 1], (lax.rem(z + k, n), q))

    for k in range(1, n):
        diag_copy(k).start()

    def add(p, carry):
        total = out_ref[p]
        for k in range(1, n):
            gram_copy(k, p).wait_recv()
            total += g_recv[k - 1, p].astype(jnp.float32)
        out_ref[p] = total
        return carry

    lax.fori_loop(0, pairs, add, 0)
    for k in range(1, n):
        diag_copy(k).wait_recv()

    slab_row = lax.broadcasted_iota(jnp.int32, (slab, width), 0) + z * slab
    slab_col = lax.broadcasted_iota(jnp.int32, (slab, width), 1)
    last = jnp.maximum(slab_row, slab_col)

    def close(p, carry):
        diag = d_own[p]
        for k in range(1, n):
            diag += d_recv[k - 1, p]
        value = jnp.where(slab_row == slab_col, diag, out_ref[p])
        out_ref[p] = jnp.where(last < cnt_ref[p] * rows, value, 0.0)
        return carry

    lax.fori_loop(0, pairs, close, 0)

    def drain(c, carry):
        for right in (True, False):
            for h in range(n - 1):
                goes = (has_right & (z - h >= 0)) if right else (has_left & (z + h < n))

                @pl.when(goes)
                def _():
                    along(h, c, right).wait_send()
        for k in range(chips):
            spread(k, c).wait_send()
        for k in range(1, chips):
            forward(k, c).wait_send()
        return carry

    lax.fori_loop(0, chunks, drain, 0)

    def drain_gram(p, carry):
        for k in range(1, n):
            gram_copy(k, p).wait_send()
        return carry

    lax.fori_loop(0, pairs, drain_gram, 0)
    for k in range(1, n):
        diag_copy(k).wait_send()


def per_device(n, n_pair, b_three, metric, aux_map, domains, counts):
    rows_dev, aux_dev = b_three.shape
    blocks_dev, aux_blocks = aux_map.shape
    width_cw = rows_dev // blocks_dev
    aux_width = aux_dev // aux_blocks
    pairs = counts.shape[0]
    slots = domains.shape[1]
    width = slots * width_cw
    slab = width // n
    columns = metric.shape[1]
    chips = n_pair // 2
    mask = jnp.repeat(aux_map.astype(jnp.bfloat16), aux_width, axis=1)
    masked = b_three.reshape(blocks_dev, width_cw, aux_dev) * mask[:, None, :]
    vmem = pl.BlockSpec(memory_space=pltpu.VMEM)
    smem = pl.BlockSpec(memory_space=pltpu.SMEM)
    dma = pltpu.SemaphoreType.DMA
    return pl.pallas_call(
        functools.partial(kernel, n, n_pair),
        out_shape=jax.ShapeDtypeStruct((pairs, slab, width), jnp.float32),
        in_specs=[vmem, vmem, smem, smem],
        out_specs=vmem,
        scratch_shapes=[
            pltpu.VMEM((n, blocks_dev, width_cw, aux_dev), jnp.bfloat16),
            pltpu.VMEM((n_pair, blocks_dev, width_cw, columns), jnp.bfloat16),
            pltpu.VMEM((n, pairs, slab, width), jnp.bfloat16),
            pltpu.VMEM((n - 1, pairs, slab, width), jnp.bfloat16),
            pltpu.VMEM((pairs, 1, width), jnp.float32),
            pltpu.VMEM((n - 1, pairs, 1, width), jnp.float32),
            dma((n - 1, blocks_dev)), dma((n - 1, blocks_dev)),
            dma((n - 1, blocks_dev)), dma((n - 1, blocks_dev)),
            dma((chips, blocks_dev)), dma((chips, blocks_dev)),
            dma((chips, blocks_dev)), dma((chips, blocks_dev)),
            dma((n - 1, pairs)), dma((n - 1, pairs)),
            dma((n - 1,)), dma((n - 1,)),
        ],
        compiler_params=pltpu.CompilerParams(
            collective_id=0, has_side_effects=True, vmem_limit_bytes=60 * 1024 * 1024),
    )(masked, metric, domains, counts)


def solution(mesh):
    return jax.shard_map(
        functools.partial(per_device, mesh.shape["aux"], mesh.shape["pair"]),
        mesh=mesh,
        in_specs=(P("pair", "aux"), P(None, "aux"), P("pair", "aux"), P(), P("pair")),
        out_specs=P("pair", "aux", None),
        check_vma=False,
    )
```

```python
import functools

import jax
import jax.numpy as jnp
from jax import lax
from jax.experimental import pallas as pl
from jax.experimental.pallas import tpu as pltpu
from jax.sharding import PartitionSpec as P

MESH = pl.DeviceIdType.MESH


def kernel(n, n_pair, b_hbm, metric_hbm, map_ref, dom_ref, out_ref, diag_ref,
           b_raw, b_ref, metric_ref, in_sem, b_all, table, g_send, g_recv, d_own, d_recv,
           r_s, r_r, l_s, l_r, p_s, p_r, f_s, f_r, g_s, g_r, d_s, d_r):
    chunks, rows, depth = b_hbm.shape
    pairs, slab, width = out_ref.shape
    slots = dom_ref.shape[0]
    chips = n_pair // 2
    z = lax.axis_index("aux")
    q = lax.axis_index("pair")
    core = lax.rem(q, 2)
    chip = q // 2
    partner = q + 1 - 2 * core
    has_right = z + 1 < n
    has_left = z > 0

    def chip_at(k):
        return lax.rem(chip + k + chips, chips) * 2 + core

    load_b = pltpu.make_async_copy(b_hbm, b_raw, in_sem.at[0])
    load_metric = pltpu.make_async_copy(metric_hbm, metric_ref, in_sem.at[1])
    load_b.start()
    load_metric.start()
    barrier = pltpu.get_barrier_semaphore()
    for k in range(1, n):
        pl.semaphore_signal(barrier, inc=1, device_id=(lax.rem(z + k, n), q), device_id_type=MESH)
    for k in range(1, chips):
        pl.semaphore_signal(barrier, inc=1, device_id=(z, chip_at(k)), device_id_type=MESH)
    pl.semaphore_signal(barrier, inc=1, device_id=(z, partner), device_id_type=MESH)
    aux_blocks = map_ref.shape[1]
    spread_row = lax.broadcasted_iota(jnp.int32, (aux_blocks, depth), 0)
    spread_col = lax.broadcasted_iota(jnp.int32, (aux_blocks, depth), 1) // (depth // aux_blocks)
    keep = jnp.dot(map_ref[...].astype(jnp.float32), (spread_row == spread_col).astype(jnp.float32),
                   preferred_element_type=jnp.float32)
    load_b.wait()
    for c in range(chunks):
        b_ref[c] = (b_raw[c].astype(jnp.float32) * keep[c:c + 1, :]).astype(b_ref.dtype)
    pl.semaphore_wait(barrier, n + chips - 1)

    def remote(src, dst, send, recv, device):
        return pltpu.make_async_remote_copy(
            src_ref=src, dst_ref=dst, send_sem=send, recv_sem=recv, device_id=device, device_id_type=MESH)

    def along(h, c, right):
        step = 1 if right else -1
        origin = z - step * h
        send, recv = (r_s, r_r) if right else (l_s, l_r)
        src = b_ref.at[c] if h == 0 else b_all.at[origin, c]
        return remote(src, b_all.at[origin, c], send.at[h, c], recv.at[h, c], (z + step, q))

    def arrival(h, c, right):
        recv = r_r if right else l_r
        origin = z - 1 - h if right else z + 1 + h
        return remote(b_ref.at[c], b_all.at[origin, c], recv.at[h, c], recv.at[h, c], (z, partner))

    def own_chunk(c):
        for right in (True, False):
            @pl.when(has_right if right else has_left)
            def _():
                along(0, c, right).start()

    def relay(h, c):
        for right in (True, False):
            came = z - h >= 0 if right else z + h < n

            @pl.when(came)
            def _():
                arrival(h - 1, c, right).wait_recv()

                if h < n - 1:
                    @pl.when(has_right if right else has_left)
                    def _():
                        along(h, c, right).start()

    def spread(k, c):
        target = partner if k == 0 else chip_at(k)
        return remote(table.at[q, c], table.at[q, c], p_s.at[k, c], p_r.at[k, c], (z, target))

    def forward(k, c):
        origin = chip_at(-k)
        return remote(table.at[origin, c], table.at[origin, c], f_s.at[k, c], f_r.at[k, c], (z, partner))

    def fit(c):
        total = jnp.dot(b_ref[c], metric_ref[pl.ds(pl.multiple_of(z * depth, depth), depth), :],
                        preferred_element_type=jnp.float32)
        for k in range(1, n):
            origin = lax.rem(z + k, n)
            total += jnp.dot(b_all[origin, c],
                             metric_ref[pl.ds(pl.multiple_of(origin * depth, depth), depth), :],
                             preferred_element_type=jnp.float32)
        table[q, c] = total.astype(table.dtype)
        for k in list(range(1, chips)) + [0]:
            spread(k, c).start()

    def pass_on(c):
        for k in range(1, chips):
            spread_in = remote(table.at[chip_at(-k), c], table.at[chip_at(-k), c],
                               p_s.at[k, c], p_r.at[k, c], (z, partner))
            spread_in.wait_recv()
            forward(k, c).start()

    own_chunk(0)
    load_metric.wait()

    def stage(step, carry):
        @pl.when(step + 1 < chunks)
        def _():
            own_chunk(step + 1)
        for h in range(1, n):
            @pl.when((step + 1 >= h) & (step + 1 - h < chunks))
            def _():
                relay(h, step + 1 - h)

        @pl.when((step + 2 >= n) & (step + 2 - n < chunks))
        def _():
            fit(step + 2 - n)

        @pl.when((step >= n) & (step - n < chunks))
        def _():
            pass_on(step - n)
        return carry

    lax.fori_loop(0, chunks + n, stage, 0)

    def finish(c, carry):
        remote(table.at[partner, c], table.at[partner, c], p_s.at[0, c], p_r.at[0, c],
               (z, partner)).wait_recv()
        for k in range(1, chips):
            origin = chip_at(-k) + 1 - 2 * core
            remote(table.at[origin, c], table.at[origin, c], f_s.at[k, c], f_r.at[k, c],
                   (z, partner)).wait_recv()
        return carry

    lax.fori_loop(0, chunks, finish, 0)

    row_of = lax.broadcasted_iota(jnp.int32, (width, width), 0)
    col_of = lax.broadcasted_iota(jnp.int32, (width, width), 1)

    def gram_copy(k, p):
        return remote(g_send.at[lax.rem(z + k, n), p], g_recv.at[k - 1, p],
                      g_s.at[k - 1, p], g_r.at[k - 1, p], (lax.rem(z + k, n), q))

    def gram(p, carry):
        blocks = []
        for s in range(slots):
            name = dom_ref[s, q * pairs + p]
            blocks.append(table[name // chunks, lax.rem(name, chunks)])
        stack = jnp.concatenate(blocks, axis=0)
        full = lax.dot_general(stack, stack, (((1,), (1,)), ((), ())), preferred_element_type=jnp.float32)
        d_own[p] = jnp.sum(jnp.where(row_of == col_of, full, 0.0), axis=0, keepdims=True)
        for d in range(n):
            part = full[d * slab:(d + 1) * slab]

            @pl.when(z == d)
            def _():
                out_ref[p] = part

            @pl.when(z != d)
            def _():
                g_send[d, p] = part.astype(g_send.dtype)
        for k in range(1, n):
            gram_copy(k, p).start()
        return carry

    lax.fori_loop(0, pairs, gram, 0)

    def diag_copy(k):
        return remote(d_own, d_recv.at[k - 1], d_s.at[k - 1], d_r.at[k - 1], (lax.rem(z + k, n), q))

    for k in range(1, n):
        diag_copy(k).start()

    def add(p, carry):
        total = out_ref[p]
        for k in range(1, n):
            gram_copy(k, p).wait_recv()
            total += g_recv[k - 1, p].astype(jnp.float32)
        out_ref[p] = total
        return carry

    lax.fori_loop(0, pairs, add, 0)
    for k in range(1, n):
        diag_copy(k).wait_recv()

    diag = d_own[...]
    for k in range(1, n):
        diag += d_recv[k - 1]
    diag_ref[...] = diag

    def drain(c, carry):
        for right in (True, False):
            for h in range(n - 1):
                goes = (has_right & (z - h >= 0)) if right else (has_left & (z + h < n))

                @pl.when(goes)
                def _():
                    along(h, c, right).wait_send()
        for k in range(chips):
            spread(k, c).wait_send()
        for k in range(1, chips):
            forward(k, c).wait_send()
        return carry

    lax.fori_loop(0, chunks, drain, 0)

    def drain_gram(p, carry):
        for k in range(1, n):
            gram_copy(k, p).wait_send()
        return carry

    lax.fori_loop(0, pairs, drain_gram, 0)
    for k in range(1, n):
        diag_copy(k).wait_send()


def close_kernel(rows, total_ref, diag_ref, cnt_ref, out_ref):
    pairs, slab, width = out_ref.shape
    slab_row = lax.broadcasted_iota(jnp.int32, (slab, width), 0) + lax.axis_index("aux") * slab
    slab_col = lax.broadcasted_iota(jnp.int32, (slab, width), 1)
    last = jnp.maximum(slab_row, slab_col)

    def close(p, carry):
        value = jnp.where(slab_row == slab_col, diag_ref[p], total_ref[p])
        out_ref[p] = jnp.where(last < cnt_ref[p] * rows, value, 0.0)
        return carry

    lax.fori_loop(0, pairs, close, 0)


def per_device(n, n_pair, b_three, metric, aux_map, domains, counts):
    rows_dev, aux_dev = b_three.shape
    blocks_dev, aux_blocks = aux_map.shape
    width_cw = rows_dev // blocks_dev
    pairs = counts.shape[0]
    slots = domains.shape[1]
    width = slots * width_cw
    slab = width // n
    columns = metric.shape[1]
    chips = n_pair // 2
    vmem = pl.BlockSpec(memory_space=pltpu.VMEM)
    smem = pl.BlockSpec(memory_space=pltpu.SMEM)
    dma = pltpu.SemaphoreType.DMA
    hbm = pl.BlockSpec(memory_space=pl.ANY)
    total, diag = pl.pallas_call(
        functools.partial(kernel, n, n_pair),
        out_shape=(jax.ShapeDtypeStruct((pairs, slab, width), jnp.float32),
                   jax.ShapeDtypeStruct((pairs, 1, width), jnp.float32)),
        in_specs=[hbm, hbm, vmem, smem],
        out_specs=(vmem, vmem),
        scratch_shapes=[
            pltpu.VMEM((blocks_dev, width_cw, aux_dev), jnp.bfloat16),
            pltpu.VMEM((blocks_dev, width_cw, aux_dev), jnp.bfloat16),
            pltpu.VMEM(metric.shape, jnp.bfloat16),
            dma((2,)),
            pltpu.VMEM((n, blocks_dev, width_cw, aux_dev), jnp.bfloat16),
            pltpu.VMEM((n_pair, blocks_dev, width_cw, columns), jnp.bfloat16),
            pltpu.VMEM((n, pairs, slab, width), jnp.bfloat16),
            pltpu.VMEM((n - 1, pairs, slab, width), jnp.bfloat16),
            pltpu.VMEM((pairs, 1, width), jnp.float32),
            pltpu.VMEM((n - 1, pairs, 1, width), jnp.float32),
            dma((n - 1, blocks_dev)), dma((n - 1, blocks_dev)),
            dma((n - 1, blocks_dev)), dma((n - 1, blocks_dev)),
            dma((chips, blocks_dev)), dma((chips, blocks_dev)),
            dma((chips, blocks_dev)), dma((chips, blocks_dev)),
            dma((n - 1, pairs)), dma((n - 1, pairs)),
            dma((n - 1,)), dma((n - 1,)),
        ],
        compiler_params=pltpu.CompilerParams(
            collective_id=0, has_side_effects=True, vmem_limit_bytes=60 * 1024 * 1024),
    )(b_three.reshape(blocks_dev, width_cw, aux_dev), metric, aux_map, domains.T)
    return pl.pallas_call(
        functools.partial(close_kernel, width_cw),
        out_shape=jax.ShapeDtypeStruct((pairs, slab, width), jnp.float32),
        in_specs=[vmem, vmem, smem],
        out_specs=vmem,
    )(total, diag, counts)


def solution(mesh):
    return jax.shard_map(
        functools.partial(per_device, mesh.shape["aux"], mesh.shape["pair"]),
        mesh=mesh,
        in_specs=(P("pair", "aux"), P(None, "aux"), P("pair", "aux"), P(), P("pair")),
        out_specs=P("pair", "aux", None),
        check_vma=False,
    )
```

```python
import functools

import jax
import jax.numpy as jnp
from jax import lax
from jax.experimental import pallas as pl
from jax.experimental.pallas import tpu as pltpu
from jax.sharding import PartitionSpec as P

MESH = pl.DeviceIdType.MESH


def kernel(n, n_pair, b_hbm, metric_hbm, map_ref, dom_ref, out_ref, diag_ref,
           b_raw, b_ref, metric_ref, in_sem, b_all, table, g_send, g_recv, d_own, d_recv,
           r_s, r_r, l_s, l_r, p_s, p_r, f_s, f_r, g_s, g_r, d_s, d_r, g_far, far_recv, far_send, x_s, x_r, c_s):
    chunks, rows, depth = b_hbm.shape
    pairs, slab, width = out_ref.shape
    slots = dom_ref.shape[0]
    chips = n_pair // 2
    z = lax.axis_index("aux")
    q = lax.axis_index("pair")
    core = lax.rem(q, 2)
    chip = q // 2
    partner = q + 1 - 2 * core
    has_right = z + 1 < n
    has_left = z > 0

    def chip_at(k):
        return lax.rem(chip + k + chips, chips) * 2 + core

    load_b = pltpu.make_async_copy(b_hbm, b_raw, in_sem.at[0])
    load_metric = pltpu.make_async_copy(metric_hbm, metric_ref, in_sem.at[1])
    load_b.start()
    load_metric.start()
    barrier = pltpu.get_barrier_semaphore()
    for k in range(1, n):
        pl.semaphore_signal(barrier, inc=1, device_id=(lax.rem(z + k, n), q), device_id_type=MESH)
    for k in range(1, chips):
        pl.semaphore_signal(barrier, inc=1, device_id=(z, chip_at(k)), device_id_type=MESH)
    pl.semaphore_signal(barrier, inc=1, device_id=(z, partner), device_id_type=MESH)
    aux_blocks = map_ref.shape[1]
    spread_row = lax.broadcasted_iota(jnp.int32, (aux_blocks, depth), 0)
    spread_col = lax.broadcasted_iota(jnp.int32, (aux_blocks, depth), 1) // (depth // aux_blocks)
    keep = jnp.dot(map_ref[...].astype(jnp.float32), (spread_row == spread_col).astype(jnp.float32),
                   preferred_element_type=jnp.float32)
    load_b.wait()
    for c in range(chunks):
        b_ref[c] = (b_raw[c].astype(jnp.float32) * keep[c:c + 1, :]).astype(b_ref.dtype)
    pl.semaphore_wait(barrier, n + chips - 1)

    def remote(src, dst, send, recv, device):
        return pltpu.make_async_remote_copy(
            src_ref=src, dst_ref=dst, send_sem=send, recv_sem=recv, device_id=device, device_id_type=MESH)

    def along(h, c, right):
        step = 1 if right else -1
        origin = z - step * h
        send, recv = (r_s, r_r) if right else (l_s, l_r)
        src = b_ref.at[c] if h == 0 else b_all.at[origin, c]
        return remote(src, b_all.at[origin, c], send.at[h, c], recv.at[h, c], (z + step, q))

    def arrival(h, c, right):
        recv = r_r if right else l_r
        origin = z - 1 - h if right else z + 1 + h
        return remote(b_ref.at[c], b_all.at[origin, c], recv.at[h, c], recv.at[h, c], (z, partner))

    def own_chunk(c):
        for right in (True, False):
            @pl.when(has_right if right else has_left)
            def _():
                along(0, c, right).start()

    def relay(h, c):
        for right in (True, False):
            came = z - h >= 0 if right else z + h < n

            @pl.when(came)
            def _():
                arrival(h - 1, c, right).wait_recv()

                if h < n - 1:
                    @pl.when(has_right if right else has_left)
                    def _():
                        along(h, c, right).start()

    def spread(k, c):
        target = partner if k == 0 else chip_at(k)
        return remote(table.at[q, c], table.at[q, c], p_s.at[k, c], p_r.at[k, c], (z, target))

    def forward(k, c):
        origin = chip_at(-k)
        return remote(table.at[origin, c], table.at[origin, c], f_s.at[k, c], f_r.at[k, c], (z, partner))

    def fit(c):
        total = jnp.dot(b_ref[c], metric_ref[pl.ds(pl.multiple_of(z * depth, depth), depth), :],
                        preferred_element_type=jnp.float32)
        for k in range(1, n):
            origin = lax.rem(z + k, n)
            total += jnp.dot(b_all[origin, c],
                             metric_ref[pl.ds(pl.multiple_of(origin * depth, depth), depth), :],
                             preferred_element_type=jnp.float32)
        table[q, c] = total.astype(table.dtype)
        for k in list(range(1, chips)) + [0]:
            spread(k, c).start()

    def pass_on(c):
        for k in range(1, chips):
            spread_in = remote(table.at[chip_at(-k), c], table.at[chip_at(-k), c],
                               p_s.at[k, c], p_r.at[k, c], (z, partner))
            spread_in.wait_recv()
            forward(k, c).start()

    own_chunk(0)
    load_metric.wait()

    def stage(step, carry):
        @pl.when(step + 1 < chunks)
        def _():
            own_chunk(step + 1)
        for h in range(1, n):
            @pl.when((step + 1 >= h) & (step + 1 - h < chunks))
            def _():
                relay(h, step + 1 - h)

        @pl.when((step + 2 >= n) & (step + 2 - n < chunks))
        def _():
            fit(step + 2 - n)

        @pl.when((step >= n) & (step - n < chunks))
        def _():
            pass_on(step - n)
        return carry

    lax.fori_loop(0, chunks + n, stage, 0)

    def finish(c, carry):
        remote(table.at[partner, c], table.at[partner, c], p_s.at[0, c], p_r.at[0, c],
               (z, partner)).wait_recv()
        for k in range(1, chips):
            origin = chip_at(-k) + 1 - 2 * core
            remote(table.at[origin, c], table.at[origin, c], f_s.at[k, c], f_r.at[k, c],
                   (z, partner)).wait_recv()
        return carry

    lax.fori_loop(0, chunks, finish, 0)

    row_of = lax.broadcasted_iota(jnp.int32, (width, width), 0)
    col_of = lax.broadcasted_iota(jnp.int32, (width, width), 1)

    def gram_copy(k, p):
        return remote(g_send.at[lax.rem(z + k, n), p], g_recv.at[k - 1, p],
                      g_s.at[k - 1, p], g_r.at[k - 1, p], (lax.rem(z + k, n), q))

    paired = n == 4
    is_end = (z == 0) | (z == n - 1)
    is_mid = jnp.logical_not(is_end)
    mate = z + 1 - 2 * lax.rem(z, 2)

    def mirrored(i):
        return jnp.where(z < 2, i, n - 1 - i)

    def near(p):
        return remote(g_send.at[mate, p], g_recv.at[0, p], g_s.at[0, p], g_r.at[0, p], (mate, q))

    def to_mid(j, p):
        return remote(g_send.at[mirrored(2 + j), p], far_recv.at[j, p], x_s.at[j, p], x_r.at[j, p], (mate, q))

    def across(j, p):
        return remote(far_send.at[j, p], g_recv.at[1, p], c_s.at[j, p], g_r.at[1, p], (mirrored(2 + j), q))

    def combine(p, carry):
        for j in (1, 0):
            to_mid(j, p).wait_recv()
            far_send[j, p] = (g_far[j, p] + far_recv[j, p].astype(jnp.float32)).astype(far_send.dtype)
            across(j, p).start()
        return carry

    def near_late(p, carry):
        near(p).start()
        return carry

    def gram(p, carry):
        blocks = []
        for s in range(slots):
            name = dom_ref[s, q * pairs + p]
            blocks.append(table[name // chunks, lax.rem(name, chunks)])
        stack = jnp.concatenate(blocks, axis=0)
        full = lax.dot_general(stack, stack, (((1,), (1,)), ((), ())), preferred_element_type=jnp.float32)
        d_own[p] = jnp.sum(jnp.where(row_of == col_of, full, 0.0), axis=0, keepdims=True)
        for d in range(n):
            part = full[d * slab:(d + 1) * slab]

            @pl.when(z == d)
            def _():
                out_ref[p] = part

            if paired:
                same = (z < 2) == (d < 2)

                @pl.when((z != d) & (is_end | same))
                def _():
                    g_send[d, p] = part.astype(g_send.dtype)

                @pl.when(is_mid & jnp.logical_not(same))
                def _():
                    g_far[jnp.where(z < 2, d - 2, 1 - d), p] = part
            else:
                @pl.when(z != d)
                def _():
                    g_send[d, p] = part.astype(g_send.dtype)
        if paired:
            @pl.when(is_end)
            def _():
                for j in (1, 0):
                    to_mid(j, p).start()

            @pl.when(is_mid)
            def _():
                near(p).start()
        else:
            for k in range(1, n):
                gram_copy(k, p).start()
        return carry

    lax.fori_loop(0, pairs, gram, 0)

    def diag_copy(k):
        return remote(d_own, d_recv.at[k - 1], d_s.at[k - 1], d_r.at[k - 1], (lax.rem(z + k, n), q))

    for k in range(1, n):
        diag_copy(k).start()
    if paired:
        @pl.when(is_end)
        def _():
            lax.fori_loop(0, pairs, near_late, 0)

        @pl.when(is_mid)
        def _():
            lax.fori_loop(0, pairs, combine, 0)

    def add(p, carry):
        total = out_ref[p]
        for k in range(1, 3 if paired else n):
            gram_copy(k, p).wait_recv()
            total += g_recv[k - 1, p].astype(jnp.float32)
        out_ref[p] = total
        return carry

    lax.fori_loop(0, pairs, add, 0)
    for k in range(1, n):
        diag_copy(k).wait_recv()

    diag = d_own[...]
    for k in range(1, n):
        diag += d_recv[k - 1]
    diag_ref[...] = diag

    def drain(c, carry):
        for right in (True, False):
            for h in range(n - 1):
                goes = (has_right & (z - h >= 0)) if right else (has_left & (z + h < n))

                @pl.when(goes)
                def _():
                    along(h, c, right).wait_send()
        for k in range(chips):
            spread(k, c).wait_send()
        for k in range(1, chips):
            forward(k, c).wait_send()
        return carry

    lax.fori_loop(0, chunks, drain, 0)

    def drain_gram(p, carry):
        if paired:
            near(p).wait_send()
            for j in range(2):
                @pl.when(is_end)
                def _():
                    to_mid(j, p).wait_send()

                @pl.when(is_mid)
                def _():
                    across(j, p).wait_send()
        else:
            for k in range(1, n):
                gram_copy(k, p).wait_send()
        return carry

    lax.fori_loop(0, pairs, drain_gram, 0)
    for k in range(1, n):
        diag_copy(k).wait_send()


def close_kernel(rows, total_ref, diag_ref, cnt_ref, out_ref):
    pairs, slab, width = out_ref.shape
    slab_row = lax.broadcasted_iota(jnp.int32, (slab, width), 0) + lax.axis_index("aux") * slab
    slab_col = lax.broadcasted_iota(jnp.int32, (slab, width), 1)
    last = jnp.maximum(slab_row, slab_col)

    def close(p, carry):
        value = jnp.where(slab_row == slab_col, diag_ref[p], total_ref[p])
        out_ref[p] = jnp.where(last < cnt_ref[p] * rows, value, 0.0)
        return carry

    lax.fori_loop(0, pairs, close, 0)


def per_device(n, n_pair, b_three, metric, aux_map, domains, counts):
    rows_dev, aux_dev = b_three.shape
    blocks_dev, aux_blocks = aux_map.shape
    width_cw = rows_dev // blocks_dev
    pairs = counts.shape[0]
    slots = domains.shape[1]
    width = slots * width_cw
    slab = width // n
    columns = metric.shape[1]
    chips = n_pair // 2
    far_pairs = pairs if n == 4 else 1
    vmem = pl.BlockSpec(memory_space=pltpu.VMEM)
    smem = pl.BlockSpec(memory_space=pltpu.SMEM)
    dma = pltpu.SemaphoreType.DMA
    hbm = pl.BlockSpec(memory_space=pl.ANY)
    total, diag = pl.pallas_call(
        functools.partial(kernel, n, n_pair),
        out_shape=(jax.ShapeDtypeStruct((pairs, slab, width), jnp.float32),
                   jax.ShapeDtypeStruct((pairs, 1, width), jnp.float32)),
        in_specs=[hbm, hbm, vmem, smem],
        out_specs=(vmem, vmem),
        scratch_shapes=[
            pltpu.VMEM((blocks_dev, width_cw, aux_dev), jnp.bfloat16),
            pltpu.VMEM((blocks_dev, width_cw, aux_dev), jnp.bfloat16),
            pltpu.VMEM(metric.shape, jnp.bfloat16),
            dma((2,)),
            pltpu.VMEM((n, blocks_dev, width_cw, aux_dev), jnp.bfloat16),
            pltpu.VMEM((n_pair, blocks_dev, width_cw, columns), jnp.bfloat16),
            pltpu.VMEM((n, pairs, slab, width), jnp.bfloat16),
            pltpu.VMEM((n - 1, pairs, slab, width), jnp.bfloat16),
            pltpu.VMEM((pairs, 1, width), jnp.float32),
            pltpu.VMEM((n - 1, pairs, 1, width), jnp.float32),
            dma((n - 1, blocks_dev)), dma((n - 1, blocks_dev)),
            dma((n - 1, blocks_dev)), dma((n - 1, blocks_dev)),
            dma((chips, blocks_dev)), dma((chips, blocks_dev)),
            dma((chips, blocks_dev)), dma((chips, blocks_dev)),
            dma((n - 1, pairs)), dma((n - 1, pairs)),
            dma((n - 1,)), dma((n - 1,)),
            pltpu.VMEM((2, far_pairs, slab, width), jnp.float32),
            pltpu.VMEM((2, far_pairs, slab, width), jnp.bfloat16),
            pltpu.VMEM((2, far_pairs, slab, width), jnp.bfloat16),
            dma((2, far_pairs)), dma((2, far_pairs)), dma((2, far_pairs)),
        ],
        compiler_params=pltpu.CompilerParams(
            collective_id=0, has_side_effects=True, vmem_limit_bytes=60 * 1024 * 1024),
    )(b_three.reshape(blocks_dev, width_cw, aux_dev), metric, aux_map, domains.T)
    return pl.pallas_call(
        functools.partial(close_kernel, width_cw),
        out_shape=jax.ShapeDtypeStruct((pairs, slab, width), jnp.float32),
        in_specs=[vmem, vmem, smem],
        out_specs=vmem,
    )(total, diag, counts)


def solution(mesh):
    return jax.shard_map(
        functools.partial(per_device, mesh.shape["aux"], mesh.shape["pair"]),
        mesh=mesh,
        in_specs=(P("pair", "aux"), P(None, "aux"), P("pair", "aux"), P(), P("pair")),
        out_specs=P("pair", "aux", None),
        check_vma=False,
    )
```

```python
import functools

import jax
import jax.numpy as jnp
from jax import lax
from jax.experimental import pallas as pl
from jax.experimental.pallas import tpu as pltpu
from jax.sharding import PartitionSpec as P

MESH = pl.DeviceIdType.MESH


def kernel(n, n_pair, split, b_hbm, metric_hbm, map_ref, dom_ref, out_ref, diag_ref,
           b_raw, b_ref, metric_ref, in_sem, b_all, table, g_send, g_recv, d_own, d_recv,
           r_s, r_r, l_s, l_r, p_s, p_r, f_s, f_r, g_s, g_r, d_s, d_r, g_far, far_recv, far_send, x_s, x_r, c_s):
    chunks, rows, depth = b_hbm.shape
    pairs, slab, width = out_ref.shape
    slots = dom_ref.shape[0]
    chips = n_pair // 2
    z = lax.axis_index("aux")
    q = lax.axis_index("pair")
    core = lax.rem(q, 2)
    chip = q // 2
    partner = q + 1 - 2 * core
    has_right = z + 1 < n
    has_left = z > 0

    def chip_at(k):
        return lax.rem(chip + k + chips, chips) * 2 + core

    load_b = pltpu.make_async_copy(b_hbm, b_raw, in_sem.at[0])
    load_metric = pltpu.make_async_copy(metric_hbm, metric_ref, in_sem.at[1])
    load_b.start()
    load_metric.start()
    barrier = pltpu.get_barrier_semaphore()
    for near_z, there in ((z + 1, has_right), (z - 1, has_left)):
        @pl.when(there)
        def _():
            pl.semaphore_signal(barrier, inc=1, device_id=(near_z, q), device_id_type=MESH)
    for k in range(1, chips):
        pl.semaphore_signal(barrier, inc=1, device_id=(z, chip_at(k)), device_id_type=MESH)
    pl.semaphore_signal(barrier, inc=1, device_id=(z, partner), device_id_type=MESH)
    aux_blocks = map_ref.shape[1]
    spread_row = lax.broadcasted_iota(jnp.int32, (aux_blocks, depth), 0)
    spread_col = lax.broadcasted_iota(jnp.int32, (aux_blocks, depth), 1) // (depth // aux_blocks)
    keep = jnp.dot(map_ref[...].astype(jnp.float32), (spread_row == spread_col).astype(jnp.float32),
                   preferred_element_type=jnp.float32)
    load_b.wait()
    for c in range(chunks):
        b_ref[c] = (b_raw[c].astype(jnp.float32) * keep[c // split:c // split + 1, :]).astype(b_ref.dtype)
    pl.semaphore_wait(barrier, chips + has_right.astype(jnp.int32) + has_left.astype(jnp.int32))

    def remote(src, dst, send, recv, device):
        return pltpu.make_async_remote_copy(
            src_ref=src, dst_ref=dst, send_sem=send, recv_sem=recv, device_id=device, device_id_type=MESH)

    def along(h, c, right):
        step = 1 if right else -1
        origin = z - step * h
        send, recv = (r_s, r_r) if right else (l_s, l_r)
        src = b_ref.at[c] if h == 0 else b_all.at[origin, c]
        return remote(src, b_all.at[origin, c], send.at[h, c], recv.at[h, c], (z + step, q))

    def arrival(h, c, right):
        recv = r_r if right else l_r
        origin = z - 1 - h if right else z + 1 + h
        return remote(b_ref.at[c], b_all.at[origin, c], recv.at[h, c], recv.at[h, c], (z, partner))

    def own_chunk(c):
        for right in (True, False):
            @pl.when(has_right if right else has_left)
            def _():
                along(0, c, right).start()

    def relay(h, c):
        for right in (True, False):
            came = z - h >= 0 if right else z + h < n

            @pl.when(came)
            def _():
                arrival(h - 1, c, right).wait_recv()

                if h < n - 1:
                    @pl.when(has_right if right else has_left)
                    def _():
                        along(h, c, right).start()

    def spread(k, c):
        target = partner if k == 0 else chip_at(k)
        return remote(table.at[q, c], table.at[q, c], p_s.at[k, c], p_r.at[k, c], (z, target))

    def forward(k, c):
        origin = chip_at(-k)
        return remote(table.at[origin, c], table.at[origin, c], f_s.at[k, c], f_r.at[k, c], (z, partner))

    def fit(c):
        total = jnp.dot(b_ref[c], metric_ref[pl.ds(pl.multiple_of(z * depth, depth), depth), :],
                        preferred_element_type=jnp.float32)
        for k in range(1, n):
            origin = lax.rem(z + k, n)
            total += jnp.dot(b_all[origin, c],
                             metric_ref[pl.ds(pl.multiple_of(origin * depth, depth), depth), :],
                             preferred_element_type=jnp.float32)
        table[q, c] = total.astype(table.dtype)
        for k in list(range(1, chips)) + [0]:
            spread(k, c).start()

    def pass_on(c):
        for k in range(1, chips):
            spread_in = remote(table.at[chip_at(-k), c], table.at[chip_at(-k), c],
                               p_s.at[k, c], p_r.at[k, c], (z, partner))
            spread_in.wait_recv()
            forward(k, c).start()

    own_chunk(0)
    load_metric.wait()

    def stage(step, carry):
        @pl.when(step + 1 < chunks)
        def _():
            own_chunk(step + 1)
        for h in range(1, n):
            @pl.when((step + 1 >= h) & (step + 1 - h < chunks))
            def _():
                relay(h, step + 1 - h)

        @pl.when((step + 2 >= n) & (step + 2 - n < chunks))
        def _():
            fit(step + 2 - n)

        @pl.when((step >= n) & (step - n < chunks))
        def _():
            pass_on(step - n)
        return carry

    lax.fori_loop(0, chunks + n, stage, 0)

    def finish(c, carry):
        remote(table.at[partner, c], table.at[partner, c], p_s.at[0, c], p_r.at[0, c],
               (z, partner)).wait_recv()
        for k in range(1, chips):
            origin = chip_at(-k) + 1 - 2 * core
            remote(table.at[origin, c], table.at[origin, c], f_s.at[k, c], f_r.at[k, c],
                   (z, partner)).wait_recv()
        return carry

    lax.fori_loop(0, chunks, finish, 0)

    row_of = lax.broadcasted_iota(jnp.int32, (width, width), 0)
    col_of = lax.broadcasted_iota(jnp.int32, (width, width), 1)

    def gram_copy(k, p):
        return remote(g_send.at[lax.rem(z + k, n), p], g_recv.at[k - 1, p],
                      g_s.at[k - 1, p], g_r.at[k - 1, p], (lax.rem(z + k, n), q))

    paired = n == 4
    is_end = (z == 0) | (z == n - 1)
    is_mid = jnp.logical_not(is_end)
    mate = z + 1 - 2 * lax.rem(z, 2)

    def mirrored(i):
        return jnp.where(z < 2, i, n - 1 - i)

    def near(p):
        return remote(g_send.at[mate, p], g_recv.at[0, p], g_s.at[0, p], g_r.at[0, p], (mate, q))

    def to_mid(j, p):
        return remote(g_send.at[mirrored(2 + j), p], far_recv.at[j, p], x_s.at[j, p], x_r.at[j, p], (mate, q))

    def across(j, p):
        return remote(far_send.at[j, p], g_recv.at[1, p], c_s.at[j, p], g_r.at[1, p], (mirrored(2 + j), q))

    def combine(p, carry):
        for j in (1, 0):
            to_mid(j, p).wait_recv()
            far_send[j, p] = (g_far[j, p] + far_recv[j, p].astype(jnp.float32)).astype(far_send.dtype)
            across(j, p).start()
        return carry

    def near_late(p, carry):
        near(p).start()
        return carry

    def gram(p, carry):
        blocks = []
        for s in range(slots):
            name = dom_ref[s, q * pairs + p]
            local = lax.rem(name, chunks // split) * split
            for t in range(split):
                blocks.append(table[name // (chunks // split), local + t])
        stack = jnp.concatenate(blocks, axis=0)
        full = lax.dot_general(stack, stack, (((1,), (1,)), ((), ())), preferred_element_type=jnp.float32)
        d_own[p] = jnp.sum(jnp.where(row_of == col_of, full, 0.0), axis=0, keepdims=True)
        for d in range(n):
            part = full[d * slab:(d + 1) * slab]

            @pl.when(z == d)
            def _():
                out_ref[p] = part

            if paired:
                same = (z < 2) == (d < 2)

                @pl.when((z != d) & (is_end | same))
                def _():
                    g_send[d, p] = part.astype(g_send.dtype)

                @pl.when(is_mid & jnp.logical_not(same))
                def _():
                    g_far[jnp.where(z < 2, d - 2, 1 - d), p] = part
            else:
                @pl.when(z != d)
                def _():
                    g_send[d, p] = part.astype(g_send.dtype)
        if paired:
            @pl.when(is_end)
            def _():
                for j in (1, 0):
                    to_mid(j, p).start()

            @pl.when(is_mid)
            def _():
                near(p).start()
        else:
            for k in range(1, n):
                gram_copy(k, p).start()
        return carry

    lax.fori_loop(0, pairs, gram, 0)

    def diag_copy(k):
        return remote(d_own, d_recv.at[k - 1], d_s.at[k - 1], d_r.at[k - 1], (lax.rem(z + k, n), q))

    for k in range(1, n):
        diag_copy(k).start()
    if paired:
        @pl.when(is_end)
        def _():
            lax.fori_loop(0, pairs, near_late, 0)

        @pl.when(is_mid)
        def _():
            lax.fori_loop(0, pairs, combine, 0)

    def add(p, carry):
        total = out_ref[p]
        for k in range(1, 3 if paired else n):
            gram_copy(k, p).wait_recv()
            total += g_recv[k - 1, p].astype(jnp.float32)
        out_ref[p] = total
        return carry

    lax.fori_loop(0, pairs, add, 0)
    for k in range(1, n):
        diag_copy(k).wait_recv()

    diag = d_own[...]
    for k in range(1, n):
        diag += d_recv[k - 1]
    diag_ref[...] = diag

    def drain(c, carry):
        for right in (True, False):
            for h in range(n - 1):
                goes = (has_right & (z - h >= 0)) if right else (has_left & (z + h < n))

                @pl.when(goes)
                def _():
                    along(h, c, right).wait_send()
        for k in range(chips):
            spread(k, c).wait_send()
        for k in range(1, chips):
            forward(k, c).wait_send()
        return carry

    lax.fori_loop(0, chunks, drain, 0)

    def drain_gram(p, carry):
        if paired:
            near(p).wait_send()
            for j in range(2):
                @pl.when(is_end)
                def _():
                    to_mid(j, p).wait_send()

                @pl.when(is_mid)
                def _():
                    across(j, p).wait_send()
        else:
            for k in range(1, n):
                gram_copy(k, p).wait_send()
        return carry

    lax.fori_loop(0, pairs, drain_gram, 0)
    for k in range(1, n):
        diag_copy(k).wait_send()


def close_kernel(rows, total_ref, diag_ref, cnt_ref, out_ref):
    pairs, slab, width = out_ref.shape
    slab_row = lax.broadcasted_iota(jnp.int32, (slab, width), 0) + lax.axis_index("aux") * slab
    slab_col = lax.broadcasted_iota(jnp.int32, (slab, width), 1)
    last = jnp.maximum(slab_row, slab_col)

    def close(p, carry):
        value = jnp.where(slab_row == slab_col, diag_ref[p], total_ref[p])
        out_ref[p] = jnp.where(last < cnt_ref[p] * rows, value, 0.0)
        return carry

    lax.fori_loop(0, pairs, close, 0)


def per_device(n, n_pair, b_three, metric, aux_map, domains, counts):
    rows_dev, aux_dev = b_three.shape
    blocks_dev, aux_blocks = aux_map.shape
    width_cw = rows_dev // blocks_dev
    pairs = counts.shape[0]
    slots = domains.shape[1]
    width = slots * width_cw
    slab = width // n
    split = 2 if n == 4 else 1
    chunks = blocks_dev * split
    chunk_rows = width_cw // split
    columns = metric.shape[1]
    chips = n_pair // 2
    far_pairs = pairs if n == 4 else 1
    vmem = pl.BlockSpec(memory_space=pltpu.VMEM)
    smem = pl.BlockSpec(memory_space=pltpu.SMEM)
    dma = pltpu.SemaphoreType.DMA
    hbm = pl.BlockSpec(memory_space=pl.ANY)
    total, diag = pl.pallas_call(
        functools.partial(kernel, n, n_pair, split),
        out_shape=(jax.ShapeDtypeStruct((pairs, slab, width), jnp.float32),
                   jax.ShapeDtypeStruct((pairs, 1, width), jnp.float32)),
        in_specs=[hbm, hbm, vmem, smem],
        out_specs=(vmem, vmem),
        scratch_shapes=[
            pltpu.VMEM((chunks, chunk_rows, aux_dev), jnp.bfloat16),
            pltpu.VMEM((chunks, chunk_rows, aux_dev), jnp.bfloat16),
            pltpu.VMEM(metric.shape, jnp.bfloat16),
            dma((2,)),
            pltpu.VMEM((n, chunks, chunk_rows, aux_dev), jnp.bfloat16),
            pltpu.VMEM((n_pair, chunks, chunk_rows, columns), jnp.bfloat16),
            pltpu.VMEM((n, pairs, slab, width), jnp.bfloat16),
            pltpu.VMEM((n - 1, pairs, slab, width), jnp.bfloat16),
            pltpu.VMEM((pairs, 1, width), jnp.float32),
            pltpu.VMEM((n - 1, pairs, 1, width), jnp.float32),
            dma((n - 1, chunks)), dma((n - 1, chunks)),
            dma((n - 1, chunks)), dma((n - 1, chunks)),
            dma((chips, chunks)), dma((chips, chunks)),
            dma((chips, chunks)), dma((chips, chunks)),
            dma((n - 1, pairs)), dma((n - 1, pairs)),
            dma((n - 1,)), dma((n - 1,)),
            pltpu.VMEM((2, far_pairs, slab, width), jnp.float32),
            pltpu.VMEM((2, far_pairs, slab, width), jnp.bfloat16),
            pltpu.VMEM((2, far_pairs, slab, width), jnp.bfloat16),
            dma((2, far_pairs)), dma((2, far_pairs)), dma((2, far_pairs)),
        ],
        compiler_params=pltpu.CompilerParams(
            collective_id=0, has_side_effects=True, vmem_limit_bytes=60 * 1024 * 1024),
    )(b_three.reshape(chunks, chunk_rows, aux_dev), metric, aux_map, domains.T)
    return pl.pallas_call(
        functools.partial(close_kernel, width_cw),
        out_shape=jax.ShapeDtypeStruct((pairs, slab, width), jnp.float32),
        in_specs=[vmem, vmem, smem],
        out_specs=vmem,
    )(total, diag, counts)


def solution(mesh):
    return jax.shard_map(
        functools.partial(per_device, mesh.shape["aux"], mesh.shape["pair"]),
        mesh=mesh,
        in_specs=(P("pair", "aux"), P(None, "aux"), P("pair", "aux"), P(), P("pair")),
        out_specs=P("pair", "aux", None),
        check_vma=False,
    )
```

```python
import functools

import jax
import jax.numpy as jnp
from jax import lax
from jax.experimental import pallas as pl
from jax.experimental.pallas import tpu as pltpu
from jax.sharding import PartitionSpec as P

MESH = pl.DeviceIdType.MESH


def kernel(n, n_pair, split, b_hbm, metric_hbm, map_ref, dom_ref, out_ref, diag_ref,
           b_raw, b_ref, metric_ref, in_sem, b_all, table, g_send, g_recv, d_own, d_recv,
           r_s, r_r, l_s, l_r, p_s, p_r, f_s, f_r, g_s, g_r, d_s, d_r, g_far, far_out, far_recv, far_send, late_send, late_recv, x_s, x_r, c_s):
    chunks, rows, depth = b_hbm.shape
    pairs, slab, width = out_ref.shape
    slots = dom_ref.shape[0]
    chips = n_pair // 2
    z = lax.axis_index("aux")
    q = lax.axis_index("pair")
    core = lax.rem(q, 2)
    chip = q // 2
    partner = q + 1 - 2 * core
    has_right = z + 1 < n
    has_left = z > 0

    def chip_at(k):
        return lax.rem(chip + k + chips, chips) * 2 + core

    load_b = pltpu.make_async_copy(b_hbm, b_raw, in_sem.at[0])
    load_metric = pltpu.make_async_copy(metric_hbm, metric_ref, in_sem.at[1])
    load_b.start()
    load_metric.start()
    barrier = pltpu.get_barrier_semaphore()
    for near_z, there in ((z + 1, has_right), (z - 1, has_left)):
        @pl.when(there)
        def _():
            pl.semaphore_signal(barrier, inc=1, device_id=(near_z, q), device_id_type=MESH)
    for k in range(1, chips):
        pl.semaphore_signal(barrier, inc=1, device_id=(z, chip_at(k)), device_id_type=MESH)
    pl.semaphore_signal(barrier, inc=1, device_id=(z, partner), device_id_type=MESH)
    aux_blocks = map_ref.shape[1]
    spread_row = lax.broadcasted_iota(jnp.int32, (aux_blocks, depth), 0)
    spread_col = lax.broadcasted_iota(jnp.int32, (aux_blocks, depth), 1) // (depth // aux_blocks)
    keep = jnp.dot(map_ref[...].astype(jnp.float32), (spread_row == spread_col).astype(jnp.float32),
                   preferred_element_type=jnp.float32)
    load_b.wait()
    for c in range(chunks):
        b_ref[c] = (b_raw[c].astype(jnp.float32) * keep[c // split:c // split + 1, :]).astype(b_ref.dtype)
    pl.semaphore_wait(barrier, chips + has_right.astype(jnp.int32) + has_left.astype(jnp.int32))

    def remote(src, dst, send, recv, device):
        return pltpu.make_async_remote_copy(
            src_ref=src, dst_ref=dst, send_sem=send, recv_sem=recv, device_id=device, device_id_type=MESH)

    def along(h, c, right):
        step = 1 if right else -1
        origin = z - step * h
        send, recv = (r_s, r_r) if right else (l_s, l_r)
        src = b_ref.at[c] if h == 0 else b_all.at[origin, c]
        return remote(src, b_all.at[origin, c], send.at[h, c], recv.at[h, c], (z + step, q))

    def arrival(h, c, right):
        recv = r_r if right else l_r
        origin = z - 1 - h if right else z + 1 + h
        return remote(b_ref.at[c], b_all.at[origin, c], recv.at[h, c], recv.at[h, c], (z, partner))

    def own_chunk(c):
        for right in (True, False):
            @pl.when(has_right if right else has_left)
            def _():
                along(0, c, right).start()

    def relay(h, c):
        for right in (True, False):
            came = z - h >= 0 if right else z + h < n

            @pl.when(came)
            def _():
                arrival(h - 1, c, right).wait_recv()

                if h < n - 1:
                    @pl.when(has_right if right else has_left)
                    def _():
                        along(h, c, right).start()

    def spread(k, c):
        target = partner if k == 0 else chip_at(k)
        return remote(table.at[q, c], table.at[q, c], p_s.at[k, c], p_r.at[k, c], (z, target))

    def forward(k, c):
        origin = chip_at(-k)
        return remote(table.at[origin, c], table.at[origin, c], f_s.at[k, c], f_r.at[k, c], (z, partner))

    def fit(c):
        total = jnp.dot(b_ref[c], metric_ref[pl.ds(pl.multiple_of(z * depth, depth), depth), :],
                        preferred_element_type=jnp.float32)
        for k in range(1, n):
            origin = lax.rem(z + k, n)
            total += jnp.dot(b_all[origin, c],
                             metric_ref[pl.ds(pl.multiple_of(origin * depth, depth), depth), :],
                             preferred_element_type=jnp.float32)
        table[q, c] = total.astype(table.dtype)
        for k in list(range(1, chips)) + [0]:
            spread(k, c).start()

    def pass_on(c):
        for k in range(1, chips):
            spread_in = remote(table.at[chip_at(-k), c], table.at[chip_at(-k), c],
                               p_s.at[k, c], p_r.at[k, c], (z, partner))
            spread_in.wait_recv()
            forward(k, c).start()

    own_chunk(0)
    load_metric.wait()

    def stage(step, carry):
        @pl.when(step + 1 < chunks)
        def _():
            own_chunk(step + 1)
        for h in range(1, n):
            @pl.when((step + 1 >= h) & (step + 1 - h < chunks))
            def _():
                relay(h, step + 1 - h)

        @pl.when((step + 2 >= n) & (step + 2 - n < chunks))
        def _():
            fit(step + 2 - n)

        @pl.when((step >= n) & (step - n < chunks))
        def _():
            pass_on(step - n)
        return carry

    lax.fori_loop(0, chunks + n, stage, 0)

    def finish(c, carry):
        remote(table.at[partner, c], table.at[partner, c], p_s.at[0, c], p_r.at[0, c],
               (z, partner)).wait_recv()
        for k in range(1, chips):
            origin = chip_at(-k) + 1 - 2 * core
            remote(table.at[origin, c], table.at[origin, c], f_s.at[k, c], f_r.at[k, c],
                   (z, partner)).wait_recv()
        return carry

    lax.fori_loop(0, chunks, finish, 0)

    row_of = lax.broadcasted_iota(jnp.int32, (width, width), 0)
    col_of = lax.broadcasted_iota(jnp.int32, (width, width), 1)

    def gram_copy(k, p):
        return remote(g_send.at[lax.rem(z + k, n), p], g_recv.at[k - 1, p],
                      g_s.at[k - 1, p], g_r.at[k - 1, p], (lax.rem(z + k, n), q))

    paired = n == 4
    is_end = (z == 0) | (z == n - 1)
    is_mid = jnp.logical_not(is_end)
    mate = z + 1 - 2 * lax.rem(z, 2)

    half = width // 2

    def near(p):
        return remote(g_send.at[0, p], g_recv.at[0, p], g_s.at[0, p], g_r.at[0, p], (mate, q))

    def late(p):
        return remote(late_send.at[p], late_recv.at[p], g_s.at[0, p], g_r.at[0, p], (mate, q))

    def to_mid(p):
        return remote(far_out.at[p], far_recv.at[p], x_s.at[p], x_r.at[p], (mate, q))

    def across(j, p):
        return remote(far_send.at[j, p], g_recv.at[1, p], c_s.at[j, p], g_r.at[1, p],
                      (jnp.where(z < 2, 2, 0) + j, q))

    def combine(low):
        def one(p, carry):
            to_mid(p).wait_recv()
            top = far_recv[p, 0:half].astype(jnp.float32)
            bottom = far_recv[p, half:width].astype(jnp.float32)
            parts = (top.T, bottom) if low else (top, bottom.T)
            value = (g_far[p] + jnp.concatenate(parts, axis=1)).astype(far_send.dtype)
            for j in ((1, 0) if low else (0, 1)):
                far_send[j, p] = value[j * slab:(j + 1) * slab]
                across(j, p).start()
            return carry
        lax.fori_loop(0, pairs, one, 0)

    def near_late(p, carry):
        late(p).start()
        return carry

    def gram(p, carry):
        blocks = []
        for s in range(slots):
            name = dom_ref[s, q * pairs + p]
            local = lax.rem(name, chunks // split) * split
            for t in range(split):
                blocks.append(table[name // (chunks // split), local + t])
        stack = jnp.concatenate(blocks, axis=0)
        full = lax.dot_general(stack, stack, (((1,), (1,)), ((), ())), preferred_element_type=jnp.float32)
        d_own[p] = jnp.sum(jnp.where(row_of == col_of, full, 0.0), axis=0, keepdims=True)
        for d in range(n):
            part = full[d * slab:(d + 1) * slab]

            @pl.when(z == d)
            def _():
                out_ref[p] = part

            if not paired:
                @pl.when(z != d)
                def _():
                    g_send[d, p] = part.astype(g_send.dtype)
        if paired:
            for end, low in ((0, True), (3, False)):
                near_cols, far_cols = (slice(0, half), slice(half, width))[::1 if low else -1]
                mid = 1 if low else 2

                @pl.when(z == end)
                def _():
                    far_out[p] = full[:, far_cols].astype(far_out.dtype)
                    late_send[p] = full[mid * slab:(mid + 1) * slab, near_cols].astype(late_send.dtype)
                    to_mid(p).start()

                @pl.when(z == mid)
                def _():
                    g_far[p] = full[far_cols]
                    g_send[0, p] = full[end * slab:(end + 1) * slab].astype(g_send.dtype)
                    near(p).start()
        else:
            for k in range(1, n):
                gram_copy(k, p).start()
        return carry

    lax.fori_loop(0, pairs, gram, 0)

    def diag_copy(k):
        return remote(d_own, d_recv.at[k - 1], d_s.at[k - 1], d_r.at[k - 1], (lax.rem(z + k, n), q))

    for k in range(1, n):
        diag_copy(k).start()
    if paired:
        @pl.when(is_end)
        def _():
            lax.fori_loop(0, pairs, near_late, 0)

        for mid, low in ((1, True), (2, False)):
            @pl.when(z == mid)
            def _():
                combine(low)

    def add(p, carry):
        if paired:
            remote(g_send.at[0, p], g_recv.at[1, p], g_s.at[0, p], g_r.at[1, p], (mate, q)).wait_recv()
            total = out_ref[p] + g_recv[1, p].astype(jnp.float32)

            @pl.when(is_end)
            def _():
                near(p).wait_recv()
                out_ref[p] = total + g_recv[0, p].astype(jnp.float32)

            for mid, low in ((1, True), (2, False)):
                @pl.when(z == mid)
                def _():
                    late(p).wait_recv()
                    parts = (late_recv[p], far_recv[p, mid * slab:(mid + 1) * slab])
                    whole = jnp.concatenate(parts if low else parts[::-1], axis=1)
                    out_ref[p] = total + whole.astype(jnp.float32)
            return carry
        total = out_ref[p]
        for k in range(1, n):
            gram_copy(k, p).wait_recv()
            total += g_recv[k - 1, p].astype(jnp.float32)
        out_ref[p] = total
        return carry

    lax.fori_loop(0, pairs, add, 0)
    for k in range(1, n):
        diag_copy(k).wait_recv()

    diag = d_own[...]
    for k in range(1, n):
        diag += d_recv[k - 1]
    diag_ref[...] = diag

    def drain(c, carry):
        for right in (True, False):
            for h in range(n - 1):
                goes = (has_right & (z - h >= 0)) if right else (has_left & (z + h < n))

                @pl.when(goes)
                def _():
                    along(h, c, right).wait_send()
        for k in range(chips):
            spread(k, c).wait_send()
        for k in range(1, chips):
            forward(k, c).wait_send()
        return carry

    lax.fori_loop(0, chunks, drain, 0)

    def drain_gram(p, carry):
        if paired:
            @pl.when(is_end)
            def _():
                late(p).wait_send()
                to_mid(p).wait_send()

            @pl.when(is_mid)
            def _():
                near(p).wait_send()
                for j in range(2):
                    across(j, p).wait_send()
        else:
            for k in range(1, n):
                gram_copy(k, p).wait_send()
        return carry

    lax.fori_loop(0, pairs, drain_gram, 0)
    for k in range(1, n):
        diag_copy(k).wait_send()


def close_kernel(rows, total_ref, diag_ref, cnt_ref, out_ref):
    pairs, slab, width = out_ref.shape
    slab_row = lax.broadcasted_iota(jnp.int32, (slab, width), 0) + lax.axis_index("aux") * slab
    slab_col = lax.broadcasted_iota(jnp.int32, (slab, width), 1)
    last = jnp.maximum(slab_row, slab_col)

    def close(p, carry):
        value = jnp.where(slab_row == slab_col, diag_ref[p], total_ref[p])
        out_ref[p] = jnp.where(last < cnt_ref[p] * rows, value, 0.0)
        return carry

    lax.fori_loop(0, pairs, close, 0)


def per_device(n, n_pair, b_three, metric, aux_map, domains, counts):
    rows_dev, aux_dev = b_three.shape
    blocks_dev, aux_blocks = aux_map.shape
    width_cw = rows_dev // blocks_dev
    pairs = counts.shape[0]
    slots = domains.shape[1]
    width = slots * width_cw
    slab = width // n
    split = 1
    chunks = blocks_dev * split
    chunk_rows = width_cw // split
    columns = metric.shape[1]
    chips = n_pair // 2
    far_pairs = pairs if n == 4 else 1
    vmem = pl.BlockSpec(memory_space=pltpu.VMEM)
    smem = pl.BlockSpec(memory_space=pltpu.SMEM)
    dma = pltpu.SemaphoreType.DMA
    hbm = pl.BlockSpec(memory_space=pl.ANY)
    total, diag = pl.pallas_call(
        functools.partial(kernel, n, n_pair, split),
        out_shape=(jax.ShapeDtypeStruct((pairs, slab, width), jnp.float32),
                   jax.ShapeDtypeStruct((pairs, 1, width), jnp.float32)),
        in_specs=[hbm, hbm, vmem, smem],
        out_specs=(vmem, vmem),
        scratch_shapes=[
            pltpu.VMEM((chunks, chunk_rows, aux_dev), jnp.bfloat16),
            pltpu.VMEM((chunks, chunk_rows, aux_dev), jnp.bfloat16),
            pltpu.VMEM(metric.shape, jnp.bfloat16),
            dma((2,)),
            pltpu.VMEM((n, chunks, chunk_rows, aux_dev), jnp.bfloat16),
            pltpu.VMEM((n_pair, chunks, chunk_rows, columns), jnp.bfloat16),
            pltpu.VMEM((n, pairs, slab, width), jnp.bfloat16),
            pltpu.VMEM((n - 1, pairs, slab, width), jnp.bfloat16),
            pltpu.VMEM((pairs, 1, width), jnp.float32),
            pltpu.VMEM((n - 1, pairs, 1, width), jnp.float32),
            dma((n - 1, chunks)), dma((n - 1, chunks)),
            dma((n - 1, chunks)), dma((n - 1, chunks)),
            dma((chips, chunks)), dma((chips, chunks)),
            dma((chips, chunks)), dma((chips, chunks)),
            dma((n - 1, pairs)), dma((n - 1, pairs)),
            dma((n - 1,)), dma((n - 1,)),
            pltpu.VMEM((far_pairs, width // 2, width), jnp.float32),
            pltpu.VMEM((far_pairs, width, width // 2), jnp.bfloat16),
            pltpu.VMEM((far_pairs, width, width // 2), jnp.bfloat16),
            pltpu.VMEM((2, far_pairs, slab, width), jnp.bfloat16),
            pltpu.VMEM((far_pairs, slab, width // 2), jnp.bfloat16),
            pltpu.VMEM((far_pairs, slab, width // 2), jnp.bfloat16),
            dma((far_pairs,)), dma((far_pairs,)), dma((2, far_pairs)),
        ],
        compiler_params=pltpu.CompilerParams(
            collective_id=0, has_side_effects=True, vmem_limit_bytes=60 * 1024 * 1024),
    )(b_three.reshape(chunks, chunk_rows, aux_dev), metric, aux_map, domains.T)
    return pl.pallas_call(
        functools.partial(close_kernel, width_cw),
        out_shape=jax.ShapeDtypeStruct((pairs, slab, width), jnp.float32),
        in_specs=[vmem, vmem, smem],
        out_specs=vmem,
    )(total, diag, counts)


def solution(mesh):
    return jax.shard_map(
        functools.partial(per_device, mesh.shape["aux"], mesh.shape["pair"]),
        mesh=mesh,
        in_specs=(P("pair", "aux"), P(None, "aux"), P("pair", "aux"), P(), P("pair")),
        out_specs=P("pair", "aux", None),
        check_vma=False,
    )
```

```python
import functools

import jax
import jax.numpy as jnp
from jax import lax
from jax.experimental import pallas as pl
from jax.experimental.pallas import tpu as pltpu
from jax.sharding import PartitionSpec as P

MESH = pl.DeviceIdType.MESH


def kernel(n, n_pair, split, b_hbm, metric_hbm, map_ref, dom_ref, out_ref, diag_ref,
           b_raw, b_ref, metric_ref, in_sem, b_all, table, g_send, g_recv, d_own, d_recv,
           r_s, r_r, l_s, l_r, p_s, p_r, f_s, f_r, g_s, g_r, d_s, d_r, g_far, far_out, far_recv, far_send, late_send, late_recv, x_s, x_r, c_s):
    chunks, rows, depth = b_hbm.shape
    pairs, slab, width = out_ref.shape
    slots = dom_ref.shape[0]
    chips = n_pair // 2
    z = lax.axis_index("aux")
    q = lax.axis_index("pair")
    core = lax.rem(q, 2)
    chip = q // 2
    partner = q + 1 - 2 * core
    has_right = z + 1 < n
    has_left = z > 0

    def chip_at(k):
        return lax.rem(chip + k + chips, chips) * 2 + core

    load_b = pltpu.make_async_copy(b_hbm, b_raw, in_sem.at[0])
    load_metric = pltpu.make_async_copy(metric_hbm, metric_ref, in_sem.at[1])
    load_b.start()
    load_metric.start()
    barrier = pltpu.get_barrier_semaphore()
    for near_z, there in ((z + 1, has_right), (z - 1, has_left)):
        @pl.when(there)
        def _():
            pl.semaphore_signal(barrier, inc=1, device_id=(near_z, q), device_id_type=MESH)
    for k in range(1, chips):
        pl.semaphore_signal(barrier, inc=1, device_id=(z, chip_at(k)), device_id_type=MESH)
    pl.semaphore_signal(barrier, inc=1, device_id=(z, partner), device_id_type=MESH)
    aux_blocks = map_ref.shape[1]
    spread_row = lax.broadcasted_iota(jnp.int32, (aux_blocks, depth), 0)
    spread_col = lax.broadcasted_iota(jnp.int32, (aux_blocks, depth), 1) // (depth // aux_blocks)
    keep = jnp.dot(map_ref[...].astype(jnp.float32), (spread_row == spread_col).astype(jnp.float32),
                   preferred_element_type=jnp.float32)
    load_b.wait()
    for c in range(chunks):
        b_ref[c] = (b_raw[c].astype(jnp.float32) * keep[c // split:c // split + 1, :]).astype(b_ref.dtype)
    pl.semaphore_wait(barrier, chips + has_right.astype(jnp.int32) + has_left.astype(jnp.int32))

    def remote(src, dst, send, recv, device):
        return pltpu.make_async_remote_copy(
            src_ref=src, dst_ref=dst, send_sem=send, recv_sem=recv, device_id=device, device_id_type=MESH)

    def along(h, c, right):
        step = 1 if right else -1
        origin = z - step * h
        send, recv = (r_s, r_r) if right else (l_s, l_r)
        src = b_ref.at[c] if h == 0 else b_all.at[origin, c]
        return remote(src, b_all.at[origin, c], send.at[h, c], recv.at[h, c], (z + step, q))

    def arrival(h, c, right):
        recv = r_r if right else l_r
        origin = z - 1 - h if right else z + 1 + h
        return remote(b_ref.at[c], b_all.at[origin, c], recv.at[h, c], recv.at[h, c], (z, partner))

    def own_chunk(c):
        for right in (True, False):
            @pl.when(has_right if right else has_left)
            def _():
                along(0, c, right).start()

    def relay(h, c):
        for right in (True, False):
            came = z - h >= 0 if right else z + h < n

            @pl.when(came)
            def _():
                arrival(h - 1, c, right).wait_recv()

                if h < n - 1:
                    @pl.when(has_right if right else has_left)
                    def _():
                        along(h, c, right).start()

    def spread(k, c):
        target = partner if k == 0 else chip_at(k)
        return remote(table.at[q, c], table.at[q, c], p_s.at[k, c], p_r.at[k, c], (z, target))

    def forward(k, c):
        origin = chip_at(-k)
        return remote(table.at[origin, c], table.at[origin, c], f_s.at[k, c], f_r.at[k, c], (z, partner))

    def fit(c):
        total = jnp.dot(b_ref[c], metric_ref[pl.ds(pl.multiple_of(z * depth, depth), depth), :],
                        preferred_element_type=jnp.float32)
        for k in range(1, n):
            origin = lax.rem(z + k, n)
            total += jnp.dot(b_all[origin, c],
                             metric_ref[pl.ds(pl.multiple_of(origin * depth, depth), depth), :],
                             preferred_element_type=jnp.float32)
        table[q, c] = total.astype(table.dtype)
        for k in list(range(1, chips)) + [0]:
            spread(k, c).start()

    def pass_on(c):
        for k in range(1, chips):
            spread_in = remote(table.at[chip_at(-k), c], table.at[chip_at(-k), c],
                               p_s.at[k, c], p_r.at[k, c], (z, partner))
            spread_in.wait_recv()
            forward(k, c).start()

    own_chunk(0)
    load_metric.wait()

    def stage(step, carry):
        @pl.when(step + 1 < chunks)
        def _():
            own_chunk(step + 1)
        for h in range(n - 1, 0, -1):
            @pl.when((step + 1 >= h) & (step + 1 - h < chunks))
            def _():
                relay(h, step + 1 - h)

        @pl.when((step + 2 >= n) & (step + 2 - n < chunks))
        def _():
            fit(step + 2 - n)

        @pl.when((step >= n) & (step - n < chunks))
        def _():
            pass_on(step - n)
        return carry

    lax.fori_loop(0, chunks + n, stage, 0)

    def finish(c, carry):
        remote(table.at[partner, c], table.at[partner, c], p_s.at[0, c], p_r.at[0, c],
               (z, partner)).wait_recv()
        for k in range(1, chips):
            origin = chip_at(-k) + 1 - 2 * core
            remote(table.at[origin, c], table.at[origin, c], f_s.at[k, c], f_r.at[k, c],
                   (z, partner)).wait_recv()
        return carry

    lax.fori_loop(0, chunks, finish, 0)

    row_of = lax.broadcasted_iota(jnp.int32, (width, width), 0)
    col_of = lax.broadcasted_iota(jnp.int32, (width, width), 1)

    def gram_copy(k, p):
        return remote(g_send.at[lax.rem(z + k, n), p], g_recv.at[k - 1, p],
                      g_s.at[k - 1, p], g_r.at[k - 1, p], (lax.rem(z + k, n), q))

    paired = n == 4
    is_end = (z == 0) | (z == n - 1)
    is_mid = jnp.logical_not(is_end)
    mate = z + 1 - 2 * lax.rem(z, 2)

    half = width // 2

    def near(p):
        return remote(g_send.at[0, p], g_recv.at[0, p], g_s.at[0, p], g_r.at[0, p], (mate, q))

    def late(p):
        return remote(late_send.at[p], late_recv.at[p], g_s.at[0, p], g_r.at[0, p], (mate, q))

    def to_mid(p):
        return remote(far_out.at[p], far_recv.at[p], x_s.at[p], x_r.at[p], (mate, q))

    def across(j, p):
        return remote(far_send.at[j, p], g_recv.at[1, p], c_s.at[j, p], g_r.at[1, p],
                      (jnp.where(z < 2, 2, 0) + j, q))

    def combine(low):
        def one(p, carry):
            to_mid(p).wait_recv()
            top = far_recv[p, 0:half].astype(jnp.float32)
            bottom = far_recv[p, half:width].astype(jnp.float32)
            parts = (top.T, bottom) if low else (top, bottom.T)
            value = (g_far[p] + jnp.concatenate(parts, axis=1)).astype(far_send.dtype)
            for j in ((1, 0) if low else (0, 1)):
                far_send[j, p] = value[j * slab:(j + 1) * slab]
                across(j, p).start()
            return carry
        lax.fori_loop(0, pairs, one, 0)

    def near_late(p, carry):
        late(p).start()
        return carry

    def gram(p, carry):
        blocks = []
        for s in range(slots):
            name = dom_ref[s, q * pairs + p]
            local = lax.rem(name, chunks // split) * split
            for t in range(split):
                blocks.append(table[name // (chunks // split), local + t])
        stack = jnp.concatenate(blocks, axis=0)
        full = lax.dot_general(stack, stack, (((1,), (1,)), ((), ())), preferred_element_type=jnp.float32)
        d_own[p] = jnp.sum(jnp.where(row_of == col_of, full, 0.0), axis=0, keepdims=True)
        for d in range(n):
            part = full[d * slab:(d + 1) * slab]

            @pl.when(z == d)
            def _():
                out_ref[p] = part

            if not paired:
                @pl.when(z != d)
                def _():
                    g_send[d, p] = part.astype(g_send.dtype)
        if paired:
            for end, low in ((0, True), (3, False)):
                near_cols, far_cols = (slice(0, half), slice(half, width))[::1 if low else -1]
                mid = 1 if low else 2

                @pl.when(z == end)
                def _():
                    far_out[p] = full[:, far_cols].astype(far_out.dtype)
                    late_send[p] = full[mid * slab:(mid + 1) * slab, near_cols].astype(late_send.dtype)
                    to_mid(p).start()

                @pl.when(z == mid)
                def _():
                    g_far[p] = full[far_cols]
                    g_send[0, p] = full[end * slab:(end + 1) * slab].astype(g_send.dtype)
                    near(p).start()
        else:
            for k in range(1, n):
                gram_copy(k, p).start()
        return carry

    lax.fori_loop(0, pairs, gram, 0)

    def diag_copy(k):
        return remote(d_own, d_recv.at[k - 1], d_s.at[k - 1], d_r.at[k - 1], (lax.rem(z + k, n), q))

    for k in range(1, n):
        diag_copy(k).start()
    if paired:
        @pl.when(is_end)
        def _():
            lax.fori_loop(0, pairs, near_late, 0)

        for mid, low in ((1, True), (2, False)):
            @pl.when(z == mid)
            def _():
                combine(low)

    def add(p, carry):
        if paired:
            remote(g_send.at[0, p], g_recv.at[1, p], g_s.at[0, p], g_r.at[1, p], (mate, q)).wait_recv()
            total = out_ref[p] + g_recv[1, p].astype(jnp.float32)

            @pl.when(is_end)
            def _():
                near(p).wait_recv()
                out_ref[p] = total + g_recv[0, p].astype(jnp.float32)

            for mid, low in ((1, True), (2, False)):
                @pl.when(z == mid)
                def _():
                    late(p).wait_recv()
                    parts = (late_recv[p], far_recv[p, mid * slab:(mid + 1) * slab])
                    whole = jnp.concatenate(parts if low else parts[::-1], axis=1)
                    out_ref[p] = total + whole.astype(jnp.float32)
            return carry
        total = out_ref[p]
        for k in range(1, n):
            gram_copy(k, p).wait_recv()
            total += g_recv[k - 1, p].astype(jnp.float32)
        out_ref[p] = total
        return carry

    lax.fori_loop(0, pairs, add, 0)
    for k in range(1, n):
        diag_copy(k).wait_recv()

    diag = d_own[...]
    for k in range(1, n):
        diag += d_recv[k - 1]
    diag_ref[...] = diag

    def drain(c, carry):
        for right in (True, False):
            for h in range(n - 1):
                goes = (has_right & (z - h >= 0)) if right else (has_left & (z + h < n))

                @pl.when(goes)
                def _():
                    along(h, c, right).wait_send()
        for k in range(chips):
            spread(k, c).wait_send()
        for k in range(1, chips):
            forward(k, c).wait_send()
        return carry

    lax.fori_loop(0, chunks, drain, 0)

    def drain_gram(p, carry):
        if paired:
            @pl.when(is_end)
            def _():
                late(p).wait_send()
                to_mid(p).wait_send()

            @pl.when(is_mid)
            def _():
                near(p).wait_send()
                for j in range(2):
                    across(j, p).wait_send()
        else:
            for k in range(1, n):
                gram_copy(k, p).wait_send()
        return carry

    lax.fori_loop(0, pairs, drain_gram, 0)
    for k in range(1, n):
        diag_copy(k).wait_send()


def close_kernel(rows, total_ref, diag_ref, cnt_ref, out_ref):
    pairs, slab, width = out_ref.shape
    slab_row = lax.broadcasted_iota(jnp.int32, (slab, width), 0) + lax.axis_index("aux") * slab
    slab_col = lax.broadcasted_iota(jnp.int32, (slab, width), 1)
    last = jnp.maximum(slab_row, slab_col)

    def close(p, carry):
        value = jnp.where(slab_row == slab_col, diag_ref[p], total_ref[p])
        out_ref[p] = jnp.where(last < cnt_ref[p] * rows, value, 0.0)
        return carry

    lax.fori_loop(0, pairs, close, 0)


def per_device(n, n_pair, b_three, metric, aux_map, domains, counts):
    rows_dev, aux_dev = b_three.shape
    blocks_dev, aux_blocks = aux_map.shape
    width_cw = rows_dev // blocks_dev
    pairs = counts.shape[0]
    slots = domains.shape[1]
    width = slots * width_cw
    slab = width // n
    split = 1
    chunks = blocks_dev * split
    chunk_rows = width_cw // split
    columns = metric.shape[1]
    chips = n_pair // 2
    far_pairs = pairs if n == 4 else 1
    vmem = pl.BlockSpec(memory_space=pltpu.VMEM)
    smem = pl.BlockSpec(memory_space=pltpu.SMEM)
    dma = pltpu.SemaphoreType.DMA
    hbm = pl.BlockSpec(memory_space=pl.ANY)
    total, diag = pl.pallas_call(
        functools.partial(kernel, n, n_pair, split),
        out_shape=(jax.ShapeDtypeStruct((pairs, slab, width), jnp.float32),
                   jax.ShapeDtypeStruct((pairs, 1, width), jnp.float32)),
        in_specs=[hbm, hbm, vmem, smem],
        out_specs=(vmem, vmem),
        scratch_shapes=[
            pltpu.VMEM((chunks, chunk_rows, aux_dev), jnp.bfloat16),
            pltpu.VMEM((chunks, chunk_rows, aux_dev), jnp.bfloat16),
            pltpu.VMEM(metric.shape, jnp.bfloat16),
            dma((2,)),
            pltpu.VMEM((n, chunks, chunk_rows, aux_dev), jnp.bfloat16),
            pltpu.VMEM((n_pair, chunks, chunk_rows, columns), jnp.bfloat16),
            pltpu.VMEM((n, pairs, slab, width), jnp.bfloat16),
            pltpu.VMEM((n - 1, pairs, slab, width), jnp.bfloat16),
            pltpu.VMEM((pairs, 1, width), jnp.float32),
            pltpu.VMEM((n - 1, pairs, 1, width), jnp.float32),
            dma((n - 1, chunks)), dma((n - 1, chunks)),
            dma((n - 1, chunks)), dma((n - 1, chunks)),
            dma((chips, chunks)), dma((chips, chunks)),
            dma((chips, chunks)), dma((chips, chunks)),
            dma((n - 1, pairs)), dma((n - 1, pairs)),
            dma((n - 1,)), dma((n - 1,)),
            pltpu.VMEM((far_pairs, width // 2, width), jnp.float32),
            pltpu.VMEM((far_pairs, width, width // 2), jnp.bfloat16),
            pltpu.VMEM((far_pairs, width, width // 2), jnp.bfloat16),
            pltpu.VMEM((2, far_pairs, slab, width), jnp.bfloat16),
            pltpu.VMEM((far_pairs, slab, width // 2), jnp.bfloat16),
            pltpu.VMEM((far_pairs, slab, width // 2), jnp.bfloat16),
            dma((far_pairs,)), dma((far_pairs,)), dma((2, far_pairs)),
        ],
        compiler_params=pltpu.CompilerParams(
            collective_id=0, has_side_effects=True, vmem_limit_bytes=60 * 1024 * 1024),
    )(b_three.reshape(chunks, chunk_rows, aux_dev), metric, aux_map, domains.T)
    return pl.pallas_call(
        functools.partial(close_kernel, width_cw),
        out_shape=jax.ShapeDtypeStruct((pairs, slab, width), jnp.float32),
        in_specs=[vmem, vmem, smem],
        out_specs=vmem,
    )(total, diag, counts)


def solution(mesh):
    return jax.shard_map(
        functools.partial(per_device, mesh.shape["aux"], mesh.shape["pair"]),
        mesh=mesh,
        in_specs=(P("pair", "aux"), P(None, "aux"), P("pair", "aux"), P(), P("pair")),
        out_specs=P("pair", "aux", None),
        check_vma=False,
    )
```

```python
import functools

import jax
import jax.numpy as jnp
from jax import lax
from jax.experimental import pallas as pl
from jax.experimental.pallas import tpu as pltpu
from jax.sharding import PartitionSpec as P

MESH = pl.DeviceIdType.MESH


def kernel(n, n_pair, split, b_hbm, metric_hbm, map_ref, dom_ref, out_ref, diag_ref,
           b_raw, b_ref, metric_ref, in_sem, b_all, table, g_send, g_recv, d_own, d_recv,
           r_s, r_r, l_s, l_r, p_s, p_r, f_s, f_r, g_s, g_r, d_s, d_r, g_far, far_out, far_recv, far_send, late_send, late_recv, x_s, x_r, c_s):
    chunks, rows, depth = b_hbm.shape
    pairs, slab, width = out_ref.shape
    slots = dom_ref.shape[0]
    chips = n_pair // 2
    z = lax.axis_index("aux")
    q = lax.axis_index("pair")
    core = lax.rem(q, 2)
    chip = q // 2
    partner = q + 1 - 2 * core
    has_right = z + 1 < n
    has_left = z > 0

    def chip_at(k):
        return lax.rem(chip + k + chips, chips) * 2 + core

    load_b = pltpu.make_async_copy(b_hbm.at[0], b_raw.at[0], in_sem.at[0])
    load_rest = pltpu.make_async_copy(b_hbm.at[1:], b_raw.at[1:], in_sem.at[2])
    load_metric = pltpu.make_async_copy(metric_hbm, metric_ref, in_sem.at[1])
    load_b.start()
    load_rest.start()
    load_metric.start()
    barrier = pltpu.get_barrier_semaphore()
    for near_z, there in ((z + 1, has_right), (z - 1, has_left)):
        @pl.when(there)
        def _():
            pl.semaphore_signal(barrier, inc=1, device_id=(near_z, q), device_id_type=MESH)
    for k in range(1, chips):
        pl.semaphore_signal(barrier, inc=1, device_id=(z, chip_at(k)), device_id_type=MESH)
    pl.semaphore_signal(barrier, inc=1, device_id=(z, partner), device_id_type=MESH)
    aux_blocks = map_ref.shape[1]
    spread_row = lax.broadcasted_iota(jnp.int32, (aux_blocks, depth), 0)
    spread_col = lax.broadcasted_iota(jnp.int32, (aux_blocks, depth), 1) // (depth // aux_blocks)
    keep = jnp.dot(map_ref[...].astype(jnp.float32), (spread_row == spread_col).astype(jnp.float32),
                   preferred_element_type=jnp.float32)
    def mask(c):
        b_ref[c] = (b_raw[c].astype(jnp.float32) * keep[c // split:c // split + 1, :]).astype(b_ref.dtype)
    load_b.wait()
    mask(0)
    pl.semaphore_wait(barrier, chips + has_right.astype(jnp.int32) + has_left.astype(jnp.int32))

    def remote(src, dst, send, recv, device):
        return pltpu.make_async_remote_copy(
            src_ref=src, dst_ref=dst, send_sem=send, recv_sem=recv, device_id=device, device_id_type=MESH)

    def along(h, c, right):
        step = 1 if right else -1
        origin = z - step * h
        send, recv = (r_s, r_r) if right else (l_s, l_r)
        src = b_ref.at[c] if h == 0 else b_all.at[origin, c]
        return remote(src, b_all.at[origin, c], send.at[h, c], recv.at[h, c], (z + step, q))

    def arrival(h, c, right):
        recv = r_r if right else l_r
        origin = z - 1 - h if right else z + 1 + h
        return remote(b_ref.at[c], b_all.at[origin, c], recv.at[h, c], recv.at[h, c], (z, partner))

    def own_chunk(c):
        for right in (True, False):
            @pl.when(has_right if right else has_left)
            def _():
                along(0, c, right).start()

    def relay(h, c):
        for right in (True, False):
            came = z - h >= 0 if right else z + h < n

            @pl.when(came)
            def _():
                arrival(h - 1, c, right).wait_recv()

                if h < n - 1:
                    @pl.when(has_right if right else has_left)
                    def _():
                        along(h, c, right).start()

    def spread(k, c):
        target = partner if k == 0 else chip_at(k)
        return remote(table.at[q, c], table.at[q, c], p_s.at[k, c], p_r.at[k, c], (z, target))

    def forward(k, c):
        origin = chip_at(-k)
        return remote(table.at[origin, c], table.at[origin, c], f_s.at[k, c], f_r.at[k, c], (z, partner))

    def fit(c):
        total = jnp.dot(b_ref[c], metric_ref[pl.ds(pl.multiple_of(z * depth, depth), depth), :],
                        preferred_element_type=jnp.float32)
        for k in range(1, n):
            origin = lax.rem(z + k, n)
            total += jnp.dot(b_all[origin, c],
                             metric_ref[pl.ds(pl.multiple_of(origin * depth, depth), depth), :],
                             preferred_element_type=jnp.float32)
        table[q, c] = total.astype(table.dtype)
        for k in list(range(1, chips)) + [0]:
            spread(k, c).start()

    def pass_on(c):
        for k in range(1, chips):
            spread_in = remote(table.at[chip_at(-k), c], table.at[chip_at(-k), c],
                               p_s.at[k, c], p_r.at[k, c], (z, partner))
            spread_in.wait_recv()
            forward(k, c).start()

    own_chunk(0)
    load_rest.wait()
    for c in range(1, chunks):
        mask(c)
    load_metric.wait()

    def stage(step, carry):
        @pl.when(step + 1 < chunks)
        def _():
            own_chunk(step + 1)
        for h in range(n - 1, 0, -1):
            @pl.when((step + 1 >= h) & (step + 1 - h < chunks))
            def _():
                relay(h, step + 1 - h)

        @pl.when((step + 2 >= n) & (step + 2 - n < chunks))
        def _():
            fit(step + 2 - n)

        @pl.when((step >= n) & (step - n < chunks))
        def _():
            pass_on(step - n)
        return carry

    lax.fori_loop(0, chunks + n, stage, 0)

    def finish(c, carry):
        remote(table.at[partner, c], table.at[partner, c], p_s.at[0, c], p_r.at[0, c],
               (z, partner)).wait_recv()
        for k in range(1, chips):
            origin = chip_at(-k) + 1 - 2 * core
            remote(table.at[origin, c], table.at[origin, c], f_s.at[k, c], f_r.at[k, c],
                   (z, partner)).wait_recv()
        return carry

    lax.fori_loop(0, chunks, finish, 0)

    row_of = lax.broadcasted_iota(jnp.int32, (width, width), 0)
    col_of = lax.broadcasted_iota(jnp.int32, (width, width), 1)

    def gram_copy(k, p):
        return remote(g_send.at[lax.rem(z + k, n), p], g_recv.at[k - 1, p],
                      g_s.at[k - 1, p], g_r.at[k - 1, p], (lax.rem(z + k, n), q))

    paired = n == 4
    is_end = (z == 0) | (z == n - 1)
    is_mid = jnp.logical_not(is_end)
    mate = z + 1 - 2 * lax.rem(z, 2)

    half = width // 2

    def near(p):
        return remote(g_send.at[0, p], g_recv.at[0, p], g_s.at[0, p], g_r.at[0, p], (mate, q))

    def late(p):
        return remote(late_send.at[p], late_recv.at[p], g_s.at[0, p], g_r.at[0, p], (mate, q))

    def to_mid(p):
        return remote(far_out.at[p], far_recv.at[p], x_s.at[p], x_r.at[p], (mate, q))

    def across(j, p):
        return remote(far_send.at[j, p], g_recv.at[1, p], c_s.at[j, p], g_r.at[1, p],
                      (jnp.where(z < 2, 2, 0) + j, q))

    def combine(low):
        def one(p, carry):
            to_mid(p).wait_recv()
            top = far_recv[p, 0:half].astype(jnp.float32)
            bottom = far_recv[p, half:width].astype(jnp.float32)
            parts = (top.T, bottom) if low else (top, bottom.T)
            value = (g_far[p] + jnp.concatenate(parts, axis=1)).astype(far_send.dtype)
            for j in ((1, 0) if low else (0, 1)):
                far_send[j, p] = value[j * slab:(j + 1) * slab]
                across(j, p).start()
            return carry
        lax.fori_loop(0, pairs, one, 0)

    def near_late(p, carry):
        late(p).start()
        return carry

    def gram(p, carry):
        blocks = []
        for s in range(slots):
            name = dom_ref[s, q * pairs + p]
            local = lax.rem(name, chunks // split) * split
            for t in range(split):
                blocks.append(table[name // (chunks // split), local + t])
        stack = jnp.concatenate(blocks, axis=0)
        full = lax.dot_general(stack, stack, (((1,), (1,)), ((), ())), preferred_element_type=jnp.float32)
        d_own[p] = jnp.sum(jnp.where(row_of == col_of, full, 0.0), axis=0, keepdims=True)
        for d in range(n):
            part = full[d * slab:(d + 1) * slab]

            @pl.when(z == d)
            def _():
                out_ref[p] = part

            if not paired:
                @pl.when(z != d)
                def _():
                    g_send[d, p] = part.astype(g_send.dtype)
        if paired:
            for end, low in ((0, True), (3, False)):
                near_cols, far_cols = (slice(0, half), slice(half, width))[::1 if low else -1]
                mid = 1 if low else 2

                @pl.when(z == end)
                def _():
                    far_out[p] = full[:, far_cols].astype(far_out.dtype)
                    late_send[p] = full[mid * slab:(mid + 1) * slab, near_cols].astype(late_send.dtype)
                    to_mid(p).start()

                @pl.when(z == mid)
                def _():
                    g_far[p] = full[far_cols]
                    g_send[0, p] = full[end * slab:(end + 1) * slab].astype(g_send.dtype)
                    near(p).start()
        else:
            for k in range(1, n):
                gram_copy(k, p).start()
        return carry

    lax.fori_loop(0, pairs, gram, 0)

    def diag_copy(k):
        return remote(d_own, d_recv.at[k - 1], d_s.at[k - 1], d_r.at[k - 1], (lax.rem(z + k, n), q))

    for k in range(1, n):
        diag_copy(k).start()
    if paired:
        @pl.when(is_end)
        def _():
            lax.fori_loop(0, pairs, near_late, 0)

        for mid, low in ((1, True), (2, False)):
            @pl.when(z == mid)
            def _():
                combine(low)

    def add(p, carry):
        if paired:
            remote(g_send.at[0, p], g_recv.at[1, p], g_s.at[0, p], g_r.at[1, p], (mate, q)).wait_recv()
            total = out_ref[p] + g_recv[1, p].astype(jnp.float32)

            @pl.when(is_end)
            def _():
                near(p).wait_recv()
                out_ref[p] = total + g_recv[0, p].astype(jnp.float32)

            for mid, low in ((1, True), (2, False)):
                @pl.when(z == mid)
                def _():
                    late(p).wait_recv()
                    parts = (late_recv[p], far_recv[p, mid * slab:(mid + 1) * slab])
                    whole = jnp.concatenate(parts if low else parts[::-1], axis=1)
                    out_ref[p] = total + whole.astype(jnp.float32)
            return carry
        total = out_ref[p]
        for k in range(1, n):
            gram_copy(k, p).wait_recv()
            total += g_recv[k - 1, p].astype(jnp.float32)
        out_ref[p] = total
        return carry

    lax.fori_loop(0, pairs, add, 0)
    for k in range(1, n):
        diag_copy(k).wait_recv()

    diag = d_own[...]
    for k in range(1, n):
        diag += d_recv[k - 1]
    diag_ref[...] = diag

    def drain(c, carry):
        for right in (True, False):
            for h in range(n - 1):
                goes = (has_right & (z - h >= 0)) if right else (has_left & (z + h < n))

                @pl.when(goes)
                def _():
                    along(h, c, right).wait_send()
        for k in range(chips):
            spread(k, c).wait_send()
        for k in range(1, chips):
            forward(k, c).wait_send()
        return carry

    lax.fori_loop(0, chunks, drain, 0)

    def drain_gram(p, carry):
        if paired:
            @pl.when(is_end)
            def _():
                late(p).wait_send()
                to_mid(p).wait_send()

            @pl.when(is_mid)
            def _():
                near(p).wait_send()
                for j in range(2):
                    across(j, p).wait_send()
        else:
            for k in range(1, n):
                gram_copy(k, p).wait_send()
        return carry

    lax.fori_loop(0, pairs, drain_gram, 0)
    for k in range(1, n):
        diag_copy(k).wait_send()


def close_kernel(rows, total_ref, diag_ref, cnt_ref, out_ref):
    pairs, slab, width = out_ref.shape
    slab_row = lax.broadcasted_iota(jnp.int32, (slab, width), 0) + lax.axis_index("aux") * slab
    slab_col = lax.broadcasted_iota(jnp.int32, (slab, width), 1)
    last = jnp.maximum(slab_row, slab_col)

    def close(p, carry):
        value = jnp.where(slab_row == slab_col, diag_ref[p], total_ref[p])
        out_ref[p] = jnp.where(last < cnt_ref[p] * rows, value, 0.0)
        return carry

    lax.fori_loop(0, pairs, close, 0)


def per_device(n, n_pair, b_three, metric, aux_map, domains, counts):
    rows_dev, aux_dev = b_three.shape
    blocks_dev, aux_blocks = aux_map.shape
    width_cw = rows_dev // blocks_dev
    pairs = counts.shape[0]
    slots = domains.shape[1]
    width = slots * width_cw
    slab = width // n
    split = 1
    chunks = blocks_dev * split
    chunk_rows = width_cw // split
    columns = metric.shape[1]
    chips = n_pair // 2
    far_pairs = pairs if n == 4 else 1
    vmem = pl.BlockSpec(memory_space=pltpu.VMEM)
    smem = pl.BlockSpec(memory_space=pltpu.SMEM)
    dma = pltpu.SemaphoreType.DMA
    hbm = pl.BlockSpec(memory_space=pl.ANY)
    total, diag = pl.pallas_call(
        functools.partial(kernel, n, n_pair, split),
        out_shape=(jax.ShapeDtypeStruct((pairs, slab, width), jnp.float32),
                   jax.ShapeDtypeStruct((pairs, 1, width), jnp.float32)),
        in_specs=[hbm, hbm, vmem, smem],
        out_specs=(vmem, vmem),
        scratch_shapes=[
            pltpu.VMEM((chunks, chunk_rows, aux_dev), jnp.bfloat16),
            pltpu.VMEM((chunks, chunk_rows, aux_dev), jnp.bfloat16),
            pltpu.VMEM(metric.shape, jnp.bfloat16),
            dma((3,)),
            pltpu.VMEM((n, chunks, chunk_rows, aux_dev), jnp.bfloat16),
            pltpu.VMEM((n_pair, chunks, chunk_rows, columns), jnp.bfloat16),
            pltpu.VMEM((n, pairs, slab, width), jnp.bfloat16),
            pltpu.VMEM((n - 1, pairs, slab, width), jnp.bfloat16),
            pltpu.VMEM((pairs, 1, width), jnp.float32),
            pltpu.VMEM((n - 1, pairs, 1, width), jnp.float32),
            dma((n - 1, chunks)), dma((n - 1, chunks)),
            dma((n - 1, chunks)), dma((n - 1, chunks)),
            dma((chips, chunks)), dma((chips, chunks)),
            dma((chips, chunks)), dma((chips, chunks)),
            dma((n - 1, pairs)), dma((n - 1, pairs)),
            dma((n - 1,)), dma((n - 1,)),
            pltpu.VMEM((far_pairs, width // 2, width), jnp.float32),
            pltpu.VMEM((far_pairs, width, width // 2), jnp.bfloat16),
            pltpu.VMEM((far_pairs, width, width // 2), jnp.bfloat16),
            pltpu.VMEM((2, far_pairs, slab, width), jnp.bfloat16),
            pltpu.VMEM((far_pairs, slab, width // 2), jnp.bfloat16),
            pltpu.VMEM((far_pairs, slab, width // 2), jnp.bfloat16),
            dma((far_pairs,)), dma((far_pairs,)), dma((2, far_pairs)),
        ],
        compiler_params=pltpu.CompilerParams(
            collective_id=0, has_side_effects=True, vmem_limit_bytes=60 * 1024 * 1024),
    )(b_three.reshape(chunks, chunk_rows, aux_dev), metric, aux_map, domains.T)
    return pl.pallas_call(
        functools.partial(close_kernel, width_cw),
        out_shape=jax.ShapeDtypeStruct((pairs, slab, width), jnp.float32),
        in_specs=[vmem, vmem, smem],
        out_specs=vmem,
    )(total, diag, counts)


def solution(mesh):
    return jax.shard_map(
        functools.partial(per_device, mesh.shape["aux"], mesh.shape["pair"]),
        mesh=mesh,
        in_specs=(P("pair", "aux"), P(None, "aux"), P("pair", "aux"), P(), P("pair")),
        out_specs=P("pair", "aux", None),
        check_vma=False,
    )
```
